32 devices in a mesh: lon: 8 (over z, x), lat: 4 (over y, core).
Axes of the slice: x: 2, y: 2, z: 4, core: 2. Of those that a mesh axis runs over, the one named last changes fastest.
Arguments:
- obs_feat: bfloat16 [32768, 128], P(('lon', 'lat')), may hold values from -6 to 6
- obs_tile: int32 [32768, 1], P(('lon', 'lat')), may hold values from 0 to 31; in each aligned block of 1024 rows (0 to 1023, 1024 to 2047, ...) at most 64 rows name the same one
- obs_cell: int32 [32768], P(('lon', 'lat')), may hold values from 0 to 4095
- w_embed: bfloat16 [128, 256], replicated, may hold values from -0.5 to 0.5
- background: bfloat16 [128, 1024, 256], P('lat', 'lon'), may hold values from -6 to 6
- w_conv: bfloat16 [9, 256, 256], replicated, may hold values from -0.125 to 0.125
- cotangent: bfloat16 [128, 1024, 256], P('lat', 'lon'), may hold values from -6 to 6
Outputs:
- encoded: bfloat16 [128, 1024, 256], P('lat', 'lon')
- record_grad: bfloat16 [32768, 256], P(('lon', 'lat'))
- conv_grad: float32 [9, 256, 256], replicated
- embed_grad: float32 [128, 256], replicated
The draws below stay inside these ranges and needn't reach their ends.
Inputs may be any that keep to these rules, and one draw needn't show every extreme that they name: `obs_tile`: among the records of one device each tile is named at most 64 times, a bound that some block reaches.
All inputs are finite; a program needn't handle non-finite values.
Results may differ from the reference program's by a relative error of at most 0.0037.
Values may be sent and summed in bfloat16 or wider, within the bound.
No kernel may reach another device: no remote copies, remote signals or barrier semaphores. Data moves between devices by JAX's collectives and lax.ppermute only.
A program may use at most 128 MiB of HBM per device.

```python
import math
import jax
import jax.numpy as jnp
import numpy as np
from jax import lax

C = 256
F = 128
CLAT = 32
CLON = 128
R_DEV = 1024
CELLS = 4096
CAP = 64
NLAT = 128
NLON = 1024
RECORDS = 32768
N_LAT = 4
DEVICES = 32


def with_ends(drawn, own_key, low, top_value):
    longest = drawn.shape.index(max(drawn.shape))
    spots = []
    for shift in (0, 1):
        where = [jax.random.randint(jax.random.fold_in(own_key, axis), (), 0, length) for axis, length in enumerate(drawn.shape)]
        where[longest] = (where[longest] + shift) % drawn.shape[longest]
        spots.append(tuple(where))
    return drawn.at[spots[0]].set(low).at[spots[1]].set(top_value)


def shard_levels(rng, dims, cuts, low, top_value):
    factor_of = 1.0
    for position, shards_of in cuts:
        draws = jax.random.uniform(jax.random.fold_in(jax.random.fold_in(rng, 6), position), (shards_of,), jnp.float32, low / len(cuts), top_value / len(cuts))
        factor_of = factor_of * jnp.repeat(jnp.exp(draws), dims[position] // shards_of).reshape((-1,) + (1,) * (len(dims) - 1 - position))
    return factor_of


def deal_out(key, own, number, rows, count, top, limit, slope):
    order = jax.random.permutation(key, count)
    crowded, usual = portions_of(count, rows * top, limit, slope, True), portions_of(count, rows * top, limit, slope, False)
    places = jnp.arange(count)

    def named(tallies, turn):
        used = int((tallies > 0).sum())
        fixed = max(1, used // 4)
        shifted = fixed + (places - fixed + turn * (used - fixed)) % max(1, count - fixed)
        return jnp.zeros((count,), jnp.int32).at[order[jnp.where(places < fixed, places, shifted)]].set(jnp.asarray(tallies, jnp.int32))

    tallies = jnp.where(number % 4 == 0, named(crowded, number // 4), named(usual, number - number // 4 - 1))
    mixed = jax.random.permutation(jax.random.fold_in(own, 3), count)
    source_of, receiver = mixed[0:count // 2 * 2:2], mixed[1:count // 2 * 2:2]
    margin = jnp.minimum(tallies[source_of] - 1, limit - tallies[receiver]) // 2
    margin = jnp.where((source_of == order[0]) | (receiver == order[0]) | (tallies[receiver] == 0), 0, jnp.maximum(margin, 0))
    shifted = jax.random.randint(jax.random.fold_in(own, 4), (count // 2,), 0, 1 << 20) % (margin + 1)
    tallies = tallies.at[source_of].add(-shifted).at[receiver].add(shifted)
    members = jnp.searchsorted(jnp.cumsum(tallies), jnp.arange(rows * top), side="right").astype(jnp.int32)
    listing = members.reshape(top, rows).T
    listing = listing[jax.random.permutation(jax.random.fold_in(own, 1), rows)]
    turn = jax.random.randint(jax.random.fold_in(own, 2), (rows, 1), 0, top)
    return jnp.take_along_axis(listing, (jnp.arange(top)[None, :] + turn) % top, axis=1)


def portions_of(count, total, limit, slope, full):
    weights = [(1 << 20) // math.isqrt(standing ** slope) + 1 for standing in range(1, count + 1)]
    largest = limit if full else min(limit, max(-(-total // count), total * weights[0] // sum(weights)))
    least = 1 if total - largest >= count - 1 else 0
    given, rest = [largest] + [least] * (count - 1), total - largest - least * (count - 1)
    while rest > 0:
        free = [i for i in range(1, count) if given[i] < largest] or [i for i in range(1, count) if given[i] < limit]
        pool, left = sum([weights[i] for i in free]), rest
        for i in free:
            addition = min(limit - given[i], max(1, left * weights[i] // pool), rest)
            given[i] = given[i] + addition
            rest = rest - addition
    return np.array(given)


def scatter_about(own_key, extent, scale, limit, pieces=(), kind=jnp.bfloat16):
    gain = shard_levels(own_key, extent, pieces, -0.22, 0.18) if pieces else 1.0
    result = jax.random.normal(own_key, extent, jnp.float32) * scale * gain
    return jnp.minimum(jnp.maximum(result, -limit), limit).astype(kind)


def setup_inputs(seed: int = 0) -> dict:
    keys = jax.random.split(jax.random.key(seed), 8)
    obs_feat = scatter_about(keys[0], (RECORDS, F), 1.0, 6.0, ((0, 32),))
    obs_tile_keys = jax.random.split(jax.random.fold_in(keys[1], 1), RECORDS // R_DEV)
    obs_tile_turns = jax.random.permutation(jax.random.fold_in(keys[1], 3), RECORDS // R_DEV)
    obs_tile = jax.vmap(lambda own, number: deal_out(jax.random.fold_in(keys[1], 2), own, number, R_DEV, DEVICES, 1, CAP, 2))(obs_tile_keys, obs_tile_turns).reshape((RECORDS, 1))
    obs_cell = with_ends(jax.random.randint(keys[2], (RECORDS,), 0, CELLS), jax.random.fold_in(keys[2], 1), 0, CELLS - 1).astype(jnp.int32)
    w_embed = scatter_about(keys[3], (F, C), F ** -0.5, 0.5)
    background = scatter_about(keys[4], (NLAT, NLON, C), 1.0, 6.0, ((0, 4), (1, 8)))
    w_conv = scatter_about(keys[5], (9, C, C), (9 * C) ** -0.5, 0.125)
    cotangent = scatter_about(keys[6], (NLAT, NLON, C), 1.0, 6.0, ((0, 4), (1, 8)))
    return dict(obs_feat=obs_feat, obs_tile=obs_tile, obs_cell=obs_cell, w_embed=w_embed, background=background, w_conv=w_conv, cotangent=cotangent)


def gelu_tanh(value):
    return jax.nn.gelu(value, approximate=True)

def reference(obs_feat, obs_tile, obs_cell, w_embed, background, w_conv, cotangent):
    hidden = jnp.dot(obs_feat, w_embed, preferred_element_type=jnp.float32)
    embed = gelu_tanh(hidden).astype(jnp.bfloat16)
    tile = obs_tile[:, 0]
    grid_row = tile % N_LAT * CLAT + obs_cell // CLON
    grid_col = tile // N_LAT * CLON + obs_cell % CLON
    aggregated = jnp.zeros((NLAT, NLON, C), jnp.float32).at[grid_row, grid_col].add(embed.astype(jnp.float32))
    field = (background.astype(jnp.float32) + aggregated).astype(jnp.bfloat16)
    field_pad = jnp.pad(jnp.pad(field, ((0, 0), (1, 1), (0, 0)), mode='wrap'), ((1, 1), (0, 0), (0, 0)))
    cot_pad = jnp.pad(jnp.pad(cotangent, ((0, 0), (1, 1), (0, 0)), mode='wrap'), ((1, 1), (0, 0), (0, 0)))
    cot_flat = cotangent.reshape(NLAT * NLON, C)
    conv = jnp.zeros((NLAT * NLON, C), jnp.float32)
    back = jnp.zeros((NLAT * NLON, C), jnp.float32)
    grads = []
    for tap in range(9):
        a, b = (tap // 3, tap % 3)
        part = field_pad[a:a + NLAT, b:b + NLON].reshape(NLAT * NLON, C)
        conv = conv + jnp.dot(part, w_conv[tap], preferred_element_type=jnp.float32)
        grads.append(lax.dot_general(part, cot_flat, (((0,), (0,)), ((), ())), preferred_element_type=jnp.float32))
        cpart = cot_pad[2 - a:2 - a + NLAT, 2 - b:2 - b + NLON].reshape(NLAT * NLON, C)
        back = back + lax.dot_general(cpart, w_conv[tap], (((1,), (1,)), ((), ())), preferred_element_type=jnp.float32)
    encoded = (field.reshape(NLAT * NLON, C).astype(jnp.float32) + conv).astype(jnp.bfloat16).reshape(NLAT, NLON, C)
    dfield = (cot_flat.astype(jnp.float32) + back).astype(jnp.bfloat16).reshape(NLAT, NLON, C)
    conv_grad = jnp.stack(grads)
    record_grad = dfield[grid_row, grid_col]
    _, pullback = jax.vjp(gelu_tanh, hidden)
    dhidden = pullback(record_grad.astype(jnp.float32))[0]
    embed_grad = jnp.dot(obs_feat.astype(jnp.float32).T, dhidden, precision=lax.Precision.HIGHEST)
    return (encoded, record_grad, conv_grad, embed_grad)
```

```python
import functools

import jax
import jax.numpy as jnp
from jax import lax
from jax.experimental import pallas as pl
from jax.experimental.pallas import tpu as pltpu
from jax.sharding import PartitionSpec as P

AXES = ("lon", "lat")
BF = jnp.bfloat16
F32 = jnp.float32
I32 = jnp.int32
VMEM_LIMIT = 56 << 20


def dot(a, b, ca=1, cb=0):
    return lax.dot_general(a, b, (((ca,), (cb,)), ((), ())), preferred_element_type=F32)


def iota(shape, dim):
    return lax.broadcasted_iota(I32, shape, dim)


def kernel_call(body, outs, args, flops=0, scratch=(), smem=(), hbm=()):
    spaces = [
        pltpu.SMEM if i in smem else pl.ANY if i in hbm else pltpu.VMEM for i in range(len(args))
    ]
    moved = sum(a.size * a.dtype.itemsize for a in args) + sum(
        o.size * o.dtype.itemsize for o in outs
    )
    return pl.pallas_call(
        body,
        out_shape=list(outs),
        in_specs=[pl.BlockSpec(memory_space=s) for s in spaces],
        out_specs=[pl.BlockSpec(memory_space=pltpu.VMEM) for _ in outs],
        scratch_shapes=list(scratch),
        compiler_params=pltpu.CompilerParams(vmem_limit_bytes=VMEM_LIMIT),
        cost_estimate=pl.CostEstimate(flops=flops, bytes_accessed=moved, transcendentals=0),
    )(*args)


def shape(dims, dtype):
    return jax.ShapeDtypeStruct(tuple(dims), dtype)


def route_body(me_ref, tile_ref, cell_ref, feat_ref, send_ref, place_ref, mask_ref, *, owners, slots):
    records = feat_ref.shape[0]
    lanes = 128
    blocks = records // lanes
    tile = tile_ref[...]
    hot = (iota((owners, records), 0) == tile).astype(F32)
    hot16 = hot.astype(BF)
    upper = (iota((lanes, lanes), 0) <= iota((lanes, lanes), 1)).astype(BF)
    carry = jnp.zeros((owners, 1), F32)
    counts = []
    for blk in range(blocks):
        local = dot(hot16[:, blk * lanes : (blk + 1) * lanes], upper)
        counts.append(local + carry)
        carry = carry + local[:, lanes - 1 : lanes]
    count = jnp.concatenate(counts, axis=1)
    rank = jnp.sum(count * hot, axis=0, keepdims=True).astype(I32) - 1
    place_ref[...] = tile * slots + rank
    shift = (me_ref[0] % (lanes // slots)) * slots
    cell = cell_ref[...]
    at = (iota((lanes, records), 0) == rank + shift).astype(BF)
    high = (hot * (cell // lanes + 1).astype(F32)).astype(BF)
    low = (hot * (cell % lanes).astype(F32)).astype(BF)
    high = dot(high, at, 1, 1)
    low = dot(low, at, 1, 1)
    zero = jnp.zeros((6, lanes), F32)
    for t in range(owners):
        extra = jnp.concatenate([high[t : t + 1], low[t : t + 1], zero], axis=0)
        send_ref[t, slots:, :] = extra.astype(BF)
    ranked = (iota((slots, records), 0) == rank).astype(BF)
    group = 512 // slots
    feat = feat_ref[...]
    for g in range(owners // group):
        for t in range(group):
            mask_ref[t * slots : (t + 1) * slots, :] = ranked * hot16[g * group + t : g * group + t + 1, :]
        rows = dot(mask_ref[...], feat).astype(BF)
        for t in range(group):
            send_ref[g * group + t, :slots, :] = rows[t * slots : (t + 1) * slots]


def unroute_body(place_ref, back_ref, out_ref):
    records = place_ref.shape[0]
    count = back_ref.shape[0]
    size = 512
    for blk in range(records // size):
        place = place_ref[blk * size : (blk + 1) * size, :]
        mask = (iota((size, count), 1) == place).astype(BF)
        out_ref[blk * size : (blk + 1) * size, :] = dot(mask, back_ref[...]).astype(BF)


def shifted(row, edge, step):
    cols = row.shape[0]
    wide = pltpu.roll(row.astype(F32), step % cols, 0)
    at = 0 if step == 1 else cols - 1
    return jnp.where(iota((cols, 1), 0) == at, edge.astype(F32), wide).astype(BF)


def fill_shifts(grid_ref, left_ref, right_ref, top_ref, bottom_ref, pad_ref):
    rows, cols, _ = grid_ref.shape

    def put(i, row, left, right):
        pad_ref[0, i] = shifted(row, left, 1)
        pad_ref[1, i] = row
        pad_ref[2, i] = shifted(row, right, -1)

    for i, ref in ((0, top_ref), (rows + 1, bottom_ref)):
        put(i, ref[0:cols, :], ref[cols : cols + 1, :], ref[cols + 8 : cols + 9, :])

    def step(i, carry):
        put(i + 1, grid_ref[i], left_ref[i], right_ref[i])
        return carry

    lax.fori_loop(0, rows, step, 0)


def conv_body(grid_ref, left_ref, right_ref, top_ref, bottom_ref, w_ref, out_ref, pad_ref, *, back):
    rows, cols, width = grid_ref.shape
    fill_shifts(grid_ref, left_ref, right_ref, top_ref, bottom_ref, pad_ref)
    high = 8

    def step(n, carry):
        i = n * high
        acc = grid_ref[pl.ds(i, high)].astype(F32).reshape(high * cols, width)
        for a in range(3):
            for b in range(3):
                part = pad_ref[b, pl.ds(i + a, high)].reshape(high * cols, width)
                tap = a * 3 + b
                acc = acc + (dot(part, w_ref[8 - tap], 1, 1) if back else dot(part, w_ref[tap]))
        out_ref[pl.ds(i, high)] = acc.astype(BF).reshape(high, cols, width)
        return carry

    lax.fori_loop(0, rows // high, step, 0)


def edges(grid):
    rows, cols, width = grid.shape
    count = lax.axis_size("lon")
    up = [(i, (i + 1) % count) for i in range(count)]
    down = [(j, i) for i, j in up]
    left = lax.ppermute(grid[:, cols - 1 :, :], "lon", up)
    right = lax.ppermute(grid[:, :1, :], "lon", down)
    count = lax.axis_size("lat")
    up = [(i, i + 1) for i in range(count - 1)]
    down = [(j, i) for i, j in up]
    pad = ((0, 7), (0, 0))

    def row(i):
        return jnp.concatenate([grid[i], jnp.pad(left[i], pad), jnp.pad(right[i], pad)], axis=0)

    top = lax.ppermute(row(rows - 1), "lat", up)
    bottom = lax.ppermute(row(0), "lat", down)
    return left, right, top, bottom


def conv(grid, halo, w, back):
    rows, cols, width = grid.shape
    outs = [shape(grid.shape, BF)]
    pad = shape((3, rows + 2, cols, width), BF)
    scratch = []
    if back:
        outs.append(pad)
    else:
        scratch.append(pltpu.VMEM(pad.shape, BF))
    flops = 18 * rows * cols * width * width
    body = functools.partial(conv_body, back=back)
    return kernel_call(body, outs, (grid, *halo, w), flops, scratch)


def gelu_parts(x):
    scale = 0.7978845608028654
    inner = scale * (x + 0.044715 * x * x * x)
    th = jnp.tanh(inner)
    value = 0.5 * x * (1.0 + th)
    slope = 0.5 * (1.0 + th) + 0.5 * x * (1.0 - th * th) * scale * (1.0 + 3 * 0.044715 * x * x)
    return value, slope


def cell_codes(recv_ref, slots):
    owners = recv_ref.shape[0]
    per = 128 // slots
    high, low = [], []
    for p in range(owners // per):
        total = recv_ref[p * per, slots : slots + 8, :].astype(F32)
        for q in range(1, per):
            total = total + recv_ref[p * per + q, slots : slots + 8, :].astype(F32)
        high.append(total[0:1])
        low.append(total[1:2])
    high = jnp.concatenate(high, axis=0)
    low = jnp.concatenate(low, axis=0)
    return (high - 1.0) * 128.0 + low


def gather_body(recv_ref, dfield_ref, w_ref, grad_ref, eg_ref, embed_ref, *, slots):
    owners = recv_ref.shape[0]
    cells = dfield_ref.shape[0]
    size = 512
    group = size // slots
    codes = cell_codes(recv_ref, slots).T.astype(I32)
    total = jnp.zeros(eg_ref.shape, F32)
    for blk in range(owners // group):
        code = jnp.concatenate([codes[:, blk * 4 + q : blk * 4 + q + 1] for q in range(4)], axis=0)
        mask = (iota((size, cells), 1) == code).astype(BF)
        rows = dot(mask, dfield_ref[...]).astype(BF)
        grad_ref[blk * size : (blk + 1) * size, :] = rows
        feat = jnp.concatenate([recv_ref[blk * group + q, :slots, :] for q in range(group)], axis=0)
        value, slope = gelu_parts(dot(feat, w_ref[...]))
        embed_ref[blk * size : (blk + 1) * size, :] = value.astype(BF)
        dh = rows.astype(F32) * slope
        part = dh.astype(BF)
        rest = (dh - part.astype(F32)).astype(BF)
        total = total + dot(feat, part, 0, 0) + dot(feat, rest, 0, 0)
    eg_ref[...] = total


def field_body(me_ref, recv_ref, embed_ref, bg_ref, pad_ref, eg_ref, field_ref, keep_ref, give_ref, acc_ref, *, slots):
    cells, width = bg_ref.shape
    cols = pad_ref.shape[2]
    half = width // 2
    codes = cell_codes(recv_ref, slots).astype(I32)
    acc_ref[...] = jnp.zeros_like(acc_ref)
    size = 512
    deep = 2 * size

    def step(n, carry):
        for k in range(deep // size):
            base = n * deep + k * size
            where = iota((size, 128), 0) + base
            mask = jnp.concatenate(
                [(where == codes[p : p + 1, :]).astype(BF) for p in range(codes.shape[0])], axis=1
            )
            at = pl.ds(pl.multiple_of(base, size), size)
            total = dot(mask, embed_ref[...]) + bg_ref[at, :].astype(F32)
            field_ref[at, :] = total.astype(BF)
        at = pl.ds(pl.multiple_of(n * deep, deep), deep)
        field = field_ref[at, :]
        high = deep // cols
        for a in range(3):
            for b in range(3):
                part = pad_ref[2 - b, pl.ds(n * high + 2 - a, high)].reshape(deep, width)
                acc_ref[3 * a + b] += dot(field, part, 0, 0)
        return carry

    lax.fori_loop(0, cells // deep, step, 0)
    side = me_ref[0] % 2
    taps = acc_ref.shape[0] * width
    inputs = eg_ref.shape[0]
    for s in range(2):
        lanes = slice(s * half, (s + 1) * half)
        for ref, want in ((keep_ref, s), (give_ref, 1 - s)):

            @pl.when(side == want)
            def _():
                for t in range(acc_ref.shape[0]):
                    ref[t * width : (t + 1) * width, :] = acc_ref[t, :, lanes]
                ref[taps : taps + inputs, :] = eg_ref[:, lanes]
                left = ref.shape[0] - taps - inputs
                if left:
                    ref[taps + inputs :, :] = jnp.zeros((left, half), F32)


def swap(x, bit):
    count = lax.axis_size("lon") * lax.axis_size("lat")
    return lax.ppermute(x, AXES, [(i, i ^ bit) for i in range(count)])


def split_body(mine_ref, *refs, moves, exact):
    terms = 0
    n = len(moves)
    ins = refs[: len(refs) - 1 - n]
    keep_ref = refs[len(refs) - 1 - n]
    outs = refs[len(refs) - n :]
    size = keep_ref.shape[0]

    def block(index):
        at = pl.ds(pl.multiple_of(index * size, 8), size)
        total = ins[0][at, :].astype(F32)
        for ref in ins[1:]:
            total = total + ref[at, :].astype(F32)
        return total

    mine = mine_ref[0]
    keep_ref[...] = block(mine).astype(keep_ref.dtype)
    for ref, move in zip(outs, moves):
        ref[...] = block(mine ^ move).astype(ref.dtype)


def join_body(mine_ref, *refs):
    out_ref = refs[-1]
    size = refs[0].shape[0]
    mine = mine_ref[0]
    for move, ref in enumerate(refs[:-1]):
        out_ref[pl.ds(pl.multiple_of((mine ^ move) * size, 8), size), :] = ref[...]


def final_body(mine_ref, own_ref, other_ref, conv_ref, embed_ref):
    side = mine_ref[0]
    half = own_ref.shape[1]
    taps, width, _ = conv_ref.shape
    inputs = embed_ref.shape[0]
    for s in range(2):
        lanes = slice(s * half, (s + 1) * half)
        for ref, want in ((own_ref, s), (other_ref, 1 - s)):

            @pl.when(side == want)
            def _():
                for t in range(taps):
                    conv_ref[t, :, lanes] = ref[t * width : (t + 1) * width, :].astype(F32)
                embed_ref[:, lanes] = ref[taps * width : taps * width + inputs, :].astype(F32)


def stages(count):
    bits, found = [], 2
    while found < count:
        bits.append(found)
        found *= 2
    return [bits[i : i + 2] for i in range(0, len(bits), 2)]


def reduce_all(me, keep, give, taps, width, inputs):
    count = lax.axis_size("lon") * lax.axis_size("lat")
    terms = [keep, swap(give, 1)]
    plan = stages(count)
    for bits in plan:
        ways = 2 ** len(bits)
        mine = (me // bits[0]) % ways
        size = terms[0].shape[0] // ways
        half = terms[0].shape[1]
        moves = list(range(1, ways))
        outs = [shape((size, half), F32)] + [shape((size, half), BF)] * len(moves)
        body = functools.partial(split_body, moves=moves, exact=False)
        own, *send = kernel_call(body, outs, (mine, *terms), smem=(0,))
        terms = [own] + [swap(x, m * bits[0]) for m, x in zip(moves, send)]
    body = functools.partial(split_body, moves=[], exact=False)
    (block,) = kernel_call(
        body, [shape(terms[0].shape, BF)], (jnp.zeros((1,), I32), *terms), smem=(0,)
    )
    for bits in reversed(plan):
        ways = 2 ** len(bits)
        mine = (me // bits[0]) % ways
        parts = [block] + [swap(block, m * bits[0]) for m in range(1, ways)]
        rows, half = block.shape
        (block,) = kernel_call(join_body, [shape((rows * ways, half), BF)], (mine, *parts), smem=(0,))
    other = swap(block, 1)
    outs = [shape((taps, width, width), F32), shape((inputs, width), F32)]
    return kernel_call(final_body, outs, (me % 2, block, other), smem=(0,))


def on_device(obs_feat, obs_tile, obs_cell, w_embed, background, w_conv, cotangent):
    lon_count = lax.axis_size("lon")
    lat_count = lax.axis_size("lat")
    owners = lon_count * lat_count
    records, inputs = obs_feat.shape
    slots = 2 * records // owners
    rows, cols, width = background.shape
    cells = rows * cols
    taps = w_conv.shape[0]
    me = (lax.axis_index("lon") * lat_count + lax.axis_index("lat")).astype(I32).reshape(1)

    outs = [shape((owners, slots + 8, inputs), BF), shape((1, records), I32)]
    send, place = kernel_call(
        functools.partial(route_body, owners=owners, slots=slots),
        outs,
        (me, obs_tile.reshape(1, records), obs_cell.reshape(1, records), obs_feat),
        flops=4 * records * records * inputs,
        scratch=[pltpu.VMEM((512, records), BF)],
        smem=(0,),
    )
    recv = lax.all_to_all(send, AXES, split_axis=0, concat_axis=0, tiled=True)

    dfield, pad = conv(cotangent, edges(cotangent), w_conv, True)

    count = owners * slots
    grad, local_eg, embed = kernel_call(
        functools.partial(gather_body, slots=slots),
        [shape((count, width), BF), shape((inputs, width), F32), shape((count, width), BF)],
        (recv, dfield.reshape(cells, width), w_embed),
        flops=2 * count * cells * width,
    )
    blocks = owners // 2
    size = 8 * blocks
    total = -(-(taps * width + inputs) // size) * size
    field, keep, give = kernel_call(
        functools.partial(field_body, slots=slots),
        [shape((cells, width), BF), shape((total, width // 2), F32), shape((total, width // 2), F32)],
        (me, recv, embed, background.reshape(cells, width), pad, local_eg),
        flops=2 * count * cells * width + 18 * cells * width * width,
        scratch=[pltpu.VMEM((taps, width, width), F32)],
        smem=(0,),
    )
    conv_grad, embed_grad = reduce_all(me, keep, give, taps, width, inputs)

    grad, field = lax.optimization_barrier((grad, field))
    back = lax.all_to_all(grad.reshape(owners, slots, width), AXES, split_axis=0, concat_axis=0, tiled=True)
    (record_grad,) = kernel_call(
        unroute_body,
        [shape((records, width), BF)],
        (place.reshape(records, 1), back.reshape(count, width)),
        flops=2 * count * records * width,
    )
    field = field.reshape(rows, cols, width)
    (encoded,) = conv(field, edges(field), w_conv, False)
    return encoded, record_grad, conv_grad, embed_grad


def solution(mesh):
    placed = (
        P(("lon", "lat"), None),
        P(("lon", "lat"), None),
        P(("lon", "lat")),
        P(),
        P("lat", "lon", None),
        P(),
        P("lat", "lon", None),
    )
    return jax.shard_map(
        on_device,
        mesh=mesh,
        in_specs=placed,
        out_specs=(P("lat", "lon", None), P(("lon", "lat"), None), P(), P()),
        check_vma=False,
    )
```

```python
import functools
import math

import jax
import jax.numpy as jnp
from jax import lax
from jax.experimental import pallas as pl
from jax.experimental.pallas import tpu as pltpu
from jax.sharding import PartitionSpec as P

AXES = ("lon", "lat")
BF = jnp.bfloat16
F32 = jnp.float32
I32 = jnp.int32


def dot(a, b, ca=1, cb=0):
    return lax.dot_general(a, b, (((ca,), (cb,)), ((), ())), preferred_element_type=F32)


def iota(shape, dim):
    return lax.broadcasted_iota(I32, shape, dim)


def kernel_call(body, outs, args, flops=0, scratch=(), smem=(), hbm=(), far=(), temp=2):
    spaces = [
        pltpu.SMEM if i in smem else pltpu.HBM if i in hbm else pltpu.VMEM for i in range(len(args))
    ]
    near = [a for i, a in enumerate(args) if i not in hbm]
    near += [o for i, o in enumerate(outs) if i not in far]
    near += [r for r in scratch if getattr(r, "memory_space", None) == pltpu.VMEM]
    held = sum(math.prod(r.shape) * r.dtype.itemsize for r in near)
    moved = sum(math.prod(r.shape) * r.dtype.itemsize for r in (*args, *outs))
    limit = (held // (1 << 20) + 1 + temp) << 20
    return pl.pallas_call(
        body,
        out_shape=[pltpu.HBM(o.shape, o.dtype) if i in far else o for i, o in enumerate(outs)],
        in_specs=[pl.BlockSpec(memory_space=s) for s in spaces],
        out_specs=[
            pl.BlockSpec(memory_space=pltpu.HBM if i in far else pltpu.VMEM) for i in range(len(outs))
        ],
        scratch_shapes=list(scratch),
        compiler_params=pltpu.CompilerParams(vmem_limit_bytes=limit),
        cost_estimate=pl.CostEstimate(flops=flops, bytes_accessed=moved, transcendentals=0),
    )(*[pltpu.with_memory_space_constraint(a, pltpu.HBM) if i in hbm else a for i, a in enumerate(args)])


def begin(src, dst, sem):
    move = pltpu.make_async_copy(src, dst, sem)
    move.start()
    return move


DMA = pltpu.SemaphoreType.DMA


def shape(dims, dtype):
    return jax.ShapeDtypeStruct(tuple(dims), dtype)


def route_body(
    me_ref, tile_hbm, cell_hbm, feat_hbm, send_ref, place_ref,
    mask_ref, tile_ref, cell_ref, feat_ref, sems, *, owners, slots,
):
    load_tile = begin(tile_hbm, tile_ref, sems.at[0])
    load_cell = begin(cell_hbm, cell_ref, sems.at[1])
    load_feat = begin(feat_hbm, feat_ref, sems.at[2])
    load_tile.wait()
    records = feat_ref.shape[0]
    lanes = 128
    blocks = records // lanes
    tile = tile_ref[...]
    hot = (iota((owners, records), 0) == tile).astype(F32)
    hot16 = hot.astype(BF)
    upper = (iota((lanes, lanes), 0) <= iota((lanes, lanes), 1)).astype(BF)
    carry = jnp.zeros((owners, 1), F32)
    counts = []
    for blk in range(blocks):
        local = dot(hot16[:, blk * lanes : (blk + 1) * lanes], upper)
        counts.append(local + carry)
        carry = carry + local[:, lanes - 1 : lanes]
    count = jnp.concatenate(counts, axis=1)
    rank = jnp.sum(count * hot, axis=0, keepdims=True).astype(I32) - 1
    place_ref[...] = tile * slots + rank
    shift = (me_ref[0] % (lanes // slots)) * slots
    load_cell.wait()
    cell = cell_ref[...]
    at = (iota((lanes, records), 0) == rank + shift).astype(BF)
    high = (hot * (cell // lanes + 1).astype(F32)).astype(BF)
    low = (hot * (cell % lanes).astype(F32)).astype(BF)
    high = dot(high, at, 1, 1)
    low = dot(low, at, 1, 1)
    zero = jnp.zeros((6, lanes), F32)
    for t in range(owners):
        extra = jnp.concatenate([high[t : t + 1], low[t : t + 1], zero], axis=0)
        send_ref[t, slots:, :] = extra.astype(BF)
    ranked = (iota((slots, records), 0) == rank).astype(BF)
    group = 512 // slots
    load_feat.wait()
    feat = feat_ref[...]
    for g in range(owners // group):
        for t in range(group):
            mask_ref[t * slots : (t + 1) * slots, :] = ranked * hot16[g * group + t : g * group + t + 1, :]
        rows = dot(mask_ref[...], feat).astype(BF)
        for t in range(group):
            send_ref[g * group + t, :slots, :] = rows[t * slots : (t + 1) * slots]


def unroute_body(place_ref, back_ref, out_ref):
    records = place_ref.shape[0]
    count = back_ref.shape[0]
    size = 512
    for blk in range(records // size):
        place = place_ref[blk * size : (blk + 1) * size, :]
        mask = (iota((size, count), 1) == place).astype(BF)
        out_ref[blk * size : (blk + 1) * size, :] = dot(mask, back_ref[...]).astype(BF)


def shifted(row, edge, step):
    cols = row.shape[0]
    wide = pltpu.roll(row.astype(F32), step % cols, 0)
    at = 0 if step == 1 else cols - 1
    return jnp.where(iota((cols, 1), 0) == at, edge.astype(F32), wide).astype(BF)


def conv_body(inside_ref, grid_hbm, left_ref, right_ref, top_ref, bottom_ref, w_hbm, *refs, back):
    if back:
        out_hbm, pad_hbm, grid_ref, w_ref, pad_ref, out_ref, in_sem, w_sem, out_sem, pad_sem = refs
    else:
        out_hbm, grid_ref, w_ref, pad_ref, out_ref, in_sem, w_sem, out_sem = refs
    rows, cols, width = grid_ref.shape
    high = 8
    blocks = rows // high

    def band(n):
        return slice(n * high, (n + 1) * high)

    loads = [begin(grid_hbm.at[band(n)], grid_ref.at[band(n)], in_sem.at[n]) for n in range(blocks)]
    load_w = begin(w_hbm, w_ref, w_sem)

    def put(i, row, left, right):
        pad_ref[0, i] = shifted(row, left, 1)
        pad_ref[1, i] = row
        pad_ref[2, i] = shifted(row, right, -1)

    for side, i, ref in ((0, 0, top_ref), (1, rows + 1, bottom_ref)):

        @pl.when(inside_ref[side] > 0)
        def _():
            put(i, ref[0:cols, :], ref[cols : cols + 1, :], ref[cols + 8 : cols + 9, :])

        @pl.when(inside_ref[side] == 0)
        def _():
            for b in range(3):
                pad_ref[b, i] = jnp.zeros(pad_ref.shape[2:], BF)

    def fill(i, carry):
        put(i + 1, grid_ref[i], left_ref[i], right_ref[i])
        return carry

    for n in range(blocks):
        loads[n].wait()
        lax.fori_loop(n * high, (n + 1) * high, fill, 0)
    stores = []
    if back:
        stores += [begin(pad_ref.at[b], pad_hbm.at[b], pad_sem.at[b]) for b in range(3)]
    load_w.wait()

    def store(n):
        some = pl.ds(n * high, high)
        return pltpu.make_async_copy(out_ref.at[some], out_hbm.at[some], out_sem.at[n])

    def step(n, carry):
        i = n * high
        acc = grid_ref[pl.ds(i, high)].astype(F32).reshape(high * cols, width)
        for a in range(3):
            for b in range(3):
                part = pad_ref[b, pl.ds(i + a, high)].reshape(high * cols, width)
                tap = a * 3 + b
                acc = acc + (dot(part, w_ref[8 - tap], 1, 1) if back else dot(part, w_ref[tap]))
        out_ref[pl.ds(i, high)] = acc.astype(BF).reshape(high, cols, width)
        store(n).start()
        return carry

    lax.fori_loop(0, blocks, step, 0)
    for n in range(blocks):
        store(n).wait()
    for move in stores:
        move.wait()


def side_edges(grid):
    cols = grid.shape[1]
    count = lax.axis_size("lon")
    up = [(i, (i + 1) % count) for i in range(count)]
    down = [(j, i) for i, j in up]
    left = lax.ppermute(grid[:, cols - 1 :, :], "lon", up)
    right = lax.ppermute(grid[:, :1, :], "lon", down)
    return left, right


def end_rows(grid, left, right):
    pad = ((0, 7), (0, 0))

    def row(i):
        return jnp.concatenate([grid[i], jnp.pad(left[i], pad), jnp.pad(right[i], pad)], axis=0)

    return row(grid.shape[0] - 1), row(0)


def end_edges(last, first):
    count = lax.axis_size("lat")
    up = [(i, (i + 1) % count) for i in range(count)]
    down = [(j, i) for i, j in up]
    return lax.ppermute(last, "lat", up), lax.ppermute(first, "lat", down)


def conv(grid, halo, w, back):
    rows, cols, width = grid.shape
    outs = [shape(grid.shape, BF)]
    pad = (3, rows + 2, cols, width)
    blocks = rows // 8
    scratch = [
        pltpu.VMEM(grid.shape, BF),
        pltpu.VMEM(w.shape, BF),
        pltpu.VMEM(pad, BF),
        pltpu.VMEM(grid.shape, BF),
        DMA((blocks,)),
        DMA,
        DMA((blocks,)),
    ]
    if back:
        outs.append(shape(pad, BF))
        scratch.append(DMA((3,)))
    flops = 18 * rows * cols * width * width
    body = functools.partial(conv_body, back=back)
    at = lax.axis_index("lat")
    inside = jnp.stack([at > 0, at < lax.axis_size("lat") - 1]).astype(I32)
    args = (inside, grid, *halo, w)
    return kernel_call(body, outs, args, flops, scratch, smem=(0,), hbm=(1, 6), far=(0, 1), temp=8)


def gelu_parts(x):
    scale = 0.7978845608028654
    inner = scale * (x + 0.044715 * x * x * x)
    th = jnp.tanh(inner)
    value = 0.5 * x * (1.0 + th)
    slope = 0.5 * (1.0 + th) + 0.5 * x * (1.0 - th * th) * scale * (1.0 + 3 * 0.044715 * x * x)
    return value, slope


def cell_codes(recv_ref, slots):
    owners = recv_ref.shape[0]
    per = 128 // slots
    high, low = [], []
    for p in range(owners // per):
        total = recv_ref[p * per, slots : slots + 8, :].astype(F32)
        for q in range(1, per):
            total = total + recv_ref[p * per + q, slots : slots + 8, :].astype(F32)
        high.append(total[0:1])
        low.append(total[1:2])
    high = jnp.concatenate(high, axis=0)
    low = jnp.concatenate(low, axis=0)
    return (high - 1.0) * 128.0 + low


def gather_body(
    recv_ref, dfield_hbm, w_ref, grad_hbm, eg_hbm, embed_hbm, code_hbm,
    dfield_ref, grad_ref, eg_ref, embed_ref, code_ref, slope_ref, in_sem, grad_sem, out_sem, *, slots,
):
    owners = recv_ref.shape[0]
    cells = dfield_ref.shape[0]
    size = 512
    group = size // slots
    blocks = owners // group
    load = begin(dfield_hbm, dfield_ref, in_sem)
    code_ref[...] = cell_codes(recv_ref, slots)
    stores = [begin(code_ref, code_hbm, out_sem.at[0])]

    def features(blk):
        return jnp.concatenate([recv_ref[blk * group + q, :slots, :] for q in range(group)], axis=0)

    for blk in range(blocks):
        at = slice(blk * size, (blk + 1) * size)
        value, slope = gelu_parts(dot(features(blk), w_ref[...]))
        embed_ref[at, :] = value.astype(BF)
        slope_ref[at, :] = slope
    stores.append(begin(embed_ref, embed_hbm, out_sem.at[1]))
    codes = code_ref[...].T.astype(I32)
    total = jnp.zeros(eg_ref.shape, F32)
    load.wait()
    for blk in range(blocks):
        at = slice(blk * size, (blk + 1) * size)
        code = jnp.concatenate([codes[:, blk * 4 + q : blk * 4 + q + 1] for q in range(4)], axis=0)
        mask = (iota((size, cells), 1) == code).astype(BF)
        rows = dot(mask, dfield_ref[...]).astype(BF)
        grad_ref[at, :] = rows
        stores.append(begin(grad_ref.at[at], grad_hbm.at[at], grad_sem.at[blk]))
        dh = rows.astype(F32) * slope_ref[at, :]
        part = dh.astype(BF)
        rest = (dh - part.astype(F32)).astype(BF)
        feat = features(blk)
        total = total + dot(feat, part, 0, 0) + dot(feat, rest, 0, 0)
    eg_ref[...] = total
    stores.append(begin(eg_ref, eg_hbm, out_sem.at[2]))
    for move in stores:
        move.wait()


def field_body(
    me_ref, code_hbm, embed_hbm, bg_hbm, pad_hbm, eg_hbm, field_hbm, keep_ref, give_ref,
    code_ref, embed_ref, bg_ref, pad_ref, eg_ref, field_ref, acc_ref, sems, pad_sems, out_sems,
):
    loads = [
        begin(code_hbm, code_ref, sems.at[0]),
        begin(embed_hbm, embed_ref, sems.at[1]),
        begin(bg_hbm, bg_ref, sems.at[2]),
        begin(pad_hbm, pad_ref, pad_sems),
        begin(eg_hbm, eg_ref, sems.at[3]),
    ]
    cells, width = bg_ref.shape
    cols = pad_ref.shape[2]
    half = width // 2
    size = 512
    deep = 2 * size
    high = deep // cols
    acc_ref[...] = jnp.zeros_like(acc_ref)
    for move in loads[:3]:
        move.wait()
    codes = code_ref[...].astype(I32)

    def store(n):
        at = pl.ds(pl.multiple_of(n * deep, deep), deep)
        return pltpu.make_async_copy(field_ref.at[at], field_hbm.at[at], out_sems.at[n])

    def scatter(n):
        for k in range(deep // size):
            base = n * deep + k * size
            where = iota((size, 128), 0) + base
            mask = jnp.concatenate(
                [(where == codes[p : p + 1, :]).astype(BF) for p in range(codes.shape[0])], axis=1
            )
            at = pl.ds(pl.multiple_of(base, size), size)
            total = dot(mask, embed_ref[...]) + bg_ref[at, :].astype(F32)
            field_ref[at, :] = total.astype(BF)
        store(n).start()

    def correlate(n):
        field = field_ref[pl.ds(pl.multiple_of(n * deep, deep), deep), :]
        for a in range(3):
            for b in range(3):
                part = pad_ref[2 - b, pl.ds(n * high + 2 - a, high)].reshape(deep, width)
                acc_ref[3 * a + b] += dot(field, part, 0, 0)

    def step(n, carry):
        scatter(n)
        correlate(n)
        return carry

    blocks = cells // deep
    scatter(0)
    loads[3].wait()
    correlate(0)
    lax.fori_loop(1, blocks, step, 0)
    loads[4].wait()
    side = me_ref[0] % 2
    taps = acc_ref.shape[0]
    used = taps * width
    inputs = eg_ref.shape[0]
    for s in range(2):
        lanes = slice(s * half, (s + 1) * half)
        for ref, want in ((keep_ref, s), (give_ref, 1 - s)):

            @pl.when(side == want)
            def _():
                for t in range(taps):
                    ref[t * width : (t + 1) * width, :] = acc_ref[t, :, lanes]
                ref[used : used + inputs, :] = eg_ref[:, lanes]
                if used + inputs < ref.shape[0]:
                    ref[used + inputs :, :] = jnp.zeros((ref.shape[0] - used - inputs, half), F32)

    for n in range(blocks):
        store(n).wait()


def swap(x, bit):
    count = lax.axis_size("lon") * lax.axis_size("lat")
    return lax.ppermute(x, AXES, [(i, i ^ bit) for i in range(count)])


def split_body(mine_ref, *refs, moves, parts):
    n = len(moves)
    ins = refs[: len(refs) - 1 - n]
    keep_ref = refs[len(refs) - 1 - n]
    outs = refs[len(refs) - n :]
    mine = mine_ref[0]

    def put(ref, index):
        row = 0
        for p in range(parts):
            terms = ins[p::parts]
            size = terms[0].shape[0] // (n + 1)
            at = pl.ds(pl.multiple_of(index * size, 8), size)
            total = terms[0][at, :].astype(F32)
            for term in terms[1:]:
                total = total + term[at, :].astype(F32)
            ref[row : row + size, :] = total.astype(ref.dtype)
            row += size

    put(keep_ref, mine)
    for ref, move in zip(outs, moves):
        put(ref, mine ^ move)


def join_body(mine_ref, *refs, parts):
    out_ref = refs[-1]
    ways = len(refs) - 1
    mine = mine_ref[0]
    for move, ref in enumerate(refs[:-1]):
        row, base = 0, 0
        for size in parts:
            at = pl.ds(pl.multiple_of(base + (mine ^ move) * size, 8), size)
            out_ref[at, :] = ref[row : row + size, :]
            row += size
            base += size * ways


def final_body(mine_ref, own_ref, other_ref, conv_ref, embed_ref):
    side = mine_ref[0]
    half = own_ref.shape[1]
    taps, width, _ = conv_ref.shape
    inputs = embed_ref.shape[0]
    for s in range(2):
        lanes = slice(s * half, (s + 1) * half)
        for ref, want in ((own_ref, s), (other_ref, 1 - s)):

            @pl.when(side == want)
            def _():
                for t in range(taps):
                    conv_ref[t, :, lanes] = ref[t * width : (t + 1) * width, :].astype(F32)
                embed_ref[:, lanes] = ref[taps * width : taps * width + inputs, :].astype(F32)


def stages(count):
    bits, found = [], 2
    while found < count:
        bits.append(found)
        found *= 2
    return [bits[i : i + 2] for i in range(0, len(bits), 2)]


def reduce_all(me, keeps, gives, taps, width, inputs, beside, encode, unroute):
    count = lax.axis_size("lon") * lax.axis_size("lat")
    terms = [*keeps, *(swap(x, 1) for x in gives)]
    half = width // 2
    plan = stages(count)
    sizes = []
    for bits in plan:
        ways = 2 ** len(bits)
        parts = len(keeps) if bits is plan[0] else 1
        sizes.append([x.shape[0] // ways for x in terms[:parts]])
        mine = (me // bits[0]) % ways
        moves = list(range(1, ways))
        outs = [shape((sum(sizes[-1]), half), F32)] + [shape((sum(sizes[-1]), half), BF)] * len(moves)
        body = functools.partial(split_body, moves=moves, parts=parts)
        own, *send = kernel_call(body, outs, (mine, *terms), smem=(0,))
        if bits is plan[0]:
            send, back = lax.optimization_barrier((send, beside[0]))
            found = encode(beside[1])
        terms = [own] + [swap(x, m * bits[0]) for m, x in zip(moves, send)]
        if bits is plan[0]:
            terms, found = lax.optimization_barrier((terms, found))
    body = functools.partial(split_body, moves=[], parts=1)
    (block,) = kernel_call(
        body, [shape(terms[0].shape, BF)], (jnp.zeros((1,), I32), *terms), smem=(0,)
    )
    for bits, parts in zip(reversed(plan), reversed(sizes)):
        ways = 2 ** len(bits)
        mine = (me // bits[0]) % ways
        pieces = [block] + [swap(block, m * bits[0]) for m in range(1, ways)]
        if bits is plan[0]:
            pieces, gone = lax.optimization_barrier((pieces, unroute(back)))
        rows = block.shape[0]
        body = functools.partial(join_body, parts=parts)
        (block,) = kernel_call(body, [shape((rows * ways, half), BF)], (mine, *pieces), smem=(0,))
    other = swap(block, 1)
    outs = [shape((taps, width, width), F32), shape((inputs, width), F32)]
    return kernel_call(final_body, outs, (me % 2, block, other), smem=(0,)), found, gone


def on_device(obs_feat, obs_tile, obs_cell, w_embed, background, w_conv, cotangent):
    lon_count = lax.axis_size("lon")
    lat_count = lax.axis_size("lat")
    owners = lon_count * lat_count
    records, inputs = obs_feat.shape
    slots = 2 * records // owners
    rows, cols, width = background.shape
    cells = rows * cols
    taps = w_conv.shape[0]
    me = (lax.axis_index("lon") * lat_count + lax.axis_index("lat")).astype(I32).reshape(1)

    outs = [shape((owners, slots + 8, inputs), BF), shape((1, records), I32)]
    send, place = kernel_call(
        functools.partial(route_body, owners=owners, slots=slots),
        outs,
        (me, obs_tile.reshape(1, records), obs_cell.reshape(1, records), obs_feat),
        flops=4 * records * records * inputs,
        scratch=[
            pltpu.VMEM((512, records), BF),
            pltpu.VMEM((1, records), I32),
            pltpu.VMEM((1, records), I32),
            pltpu.VMEM((records, inputs), BF),
            DMA((3,)),
        ],
        smem=(0,),
        hbm=(1, 2, 3),
        temp=4,
    )
    sides = side_edges(cotangent)
    send, sides = lax.optimization_barrier((send, sides))
    ends = end_rows(cotangent, *sides)
    send, ends = lax.optimization_barrier((send, ends))
    halo = (*sides, *end_edges(*ends))
    recv = lax.all_to_all(send, AXES, split_axis=0, concat_axis=0, tiled=True)

    dfield, pad = conv(cotangent, halo, w_conv, True)

    count = owners * slots
    grad, local_eg, embed, codes = kernel_call(
        functools.partial(gather_body, slots=slots),
        [
            shape((count, width), BF),
            shape((inputs, width), F32),
            shape((count, width), BF),
            shape((count // 128, 128), F32),
        ],
        (recv, dfield.reshape(cells, width), w_embed),
        flops=2 * count * cells * width,
        scratch=[
            pltpu.VMEM((cells, width), BF),
            pltpu.VMEM((count, width), BF),
            pltpu.VMEM((inputs, width), F32),
            pltpu.VMEM((count, width), BF),
            pltpu.VMEM((count // 128, 128), F32),
            pltpu.VMEM((count, width), F32),
            DMA,
            DMA((count // 512,)),
            DMA((3,)),
        ],
        hbm=(1,),
        far=(0, 1, 2, 3),
        temp=12,
    )
    blocks = owners // 2
    size = 8 * blocks
    total = -(-(taps * width + inputs) // size) * size
    back = lax.all_to_all(grad.reshape(owners, slots, width), AXES, split_axis=0, concat_axis=0, tiled=True)
    field, keep, give = kernel_call(
        field_body,
        [shape((cells, width), BF)] + [shape((total, width // 2), F32)] * 2,
        (me, codes, embed, background.reshape(cells, width), pad, local_eg),
        flops=2 * count * cells * width + 18 * cells * width * width,
        scratch=[
            pltpu.VMEM((count // 128, 128), F32),
            pltpu.VMEM((count, width), BF),
            pltpu.VMEM((cells, width), BF),
            pltpu.VMEM(pad.shape, BF),
            pltpu.VMEM((inputs, width), F32),
            pltpu.VMEM((cells, width), BF),
            pltpu.VMEM((taps, width, width), F32),
            DMA((4,)),
            DMA,
            DMA((cells // 1024,)),
        ],
        smem=(0,),
        hbm=(1, 2, 3, 4, 5),
        far=(0,),
        temp=8,
    )
    grid = field.reshape(rows, cols, width)
    sides = side_edges(grid)
    halo = (*sides, *end_edges(*end_rows(grid, *sides)))

    def encode(halo):
        return conv(grid, halo, w_conv, False)[0]

    def unroute(back):
        return kernel_call(
            unroute_body,
            [shape((records, width), BF)],
            (place.reshape(records, 1), back.reshape(count, width)),
            flops=2 * count * records * width,
            temp=4,
        )[0]

    (conv_grad, embed_grad), encoded, record_grad = reduce_all(
        me, (keep,), (give,), taps, width, inputs, (back, halo), encode, unroute
    )
    return encoded, record_grad, conv_grad, embed_grad


def solution(mesh):
    placed = (
        P(("lon", "lat"), None),
        P(("lon", "lat"), None),
        P(("lon", "lat")),
        P(),
        P("lat", "lon", None),
        P(),
        P("lat", "lon", None),
    )
    return jax.shard_map(
        on_device,
        mesh=mesh,
        in_specs=placed,
        out_specs=(P("lat", "lon", None), P(("lon", "lat"), None), P(), P()),
        check_vma=False,
    )
```

```python
import functools
import math

import jax
import jax.numpy as jnp
from jax import lax
from jax.experimental import pallas as pl
from jax.experimental.pallas import tpu as pltpu
from jax.sharding import PartitionSpec as P

AXES = ("lon", "lat")
BF = jnp.bfloat16
F32 = jnp.float32
I32 = jnp.int32


def dot(a, b, ca=1, cb=0):
    return lax.dot_general(a, b, (((ca,), (cb,)), ((), ())), preferred_element_type=F32)


def iota(shape, dim):
    return lax.broadcasted_iota(I32, shape, dim)


def kernel_call(body, outs, args, flops=0, scratch=(), smem=(), hbm=(), far=(), temp=2, alias={}):
    spaces = [
        pltpu.SMEM if i in smem else pltpu.HBM if i in hbm else pltpu.VMEM for i in range(len(args))
    ]
    near = [a for i, a in enumerate(args) if i not in hbm]
    near += [o for i, o in enumerate(outs) if i not in far]
    near += [r for r in scratch if getattr(r, "memory_space", None) == pltpu.VMEM]
    held = sum(math.prod(r.shape) * r.dtype.itemsize for r in near)
    moved = sum(math.prod(r.shape) * r.dtype.itemsize for r in (*args, *outs))
    limit = (held // (1 << 20) + 1 + temp) << 20
    return pl.pallas_call(
        body,
        out_shape=[pltpu.HBM(o.shape, o.dtype) if i in far else o for i, o in enumerate(outs)],
        in_specs=[pl.BlockSpec(memory_space=s) for s in spaces],
        out_specs=[
            pl.BlockSpec(memory_space=pltpu.HBM if i in far else pltpu.VMEM) for i in range(len(outs))
        ],
        scratch_shapes=list(scratch),
        input_output_aliases=alias,
        compiler_params=pltpu.CompilerParams(vmem_limit_bytes=limit),
        cost_estimate=pl.CostEstimate(flops=flops, bytes_accessed=moved, transcendentals=0),
    )(*[pltpu.with_memory_space_constraint(a, pltpu.HBM) if i in hbm else a for i, a in enumerate(args)])


def begin(src, dst, sem):
    move = pltpu.make_async_copy(src, dst, sem)
    move.start()
    return move


DMA = pltpu.SemaphoreType.DMA


def shape(dims, dtype):
    return jax.ShapeDtypeStruct(tuple(dims), dtype)


def route_body(
    me_ref, tile_hbm, cell_hbm, feat_hbm, send_ref, place_ref,
    mask_ref, tile_ref, cell_ref, feat_ref, sems, *, owners, slots,
):
    load_tile = begin(tile_hbm, tile_ref, sems.at[0])
    load_cell = begin(cell_hbm, cell_ref, sems.at[1])
    load_feat = begin(feat_hbm, feat_ref, sems.at[2])
    load_tile.wait()
    records = feat_ref.shape[0]
    lanes = 128
    blocks = records // lanes
    tile = tile_ref[...]
    hot = (iota((owners, records), 0) == tile).astype(F32)
    hot16 = hot.astype(BF)
    upper = (iota((lanes, lanes), 0) <= iota((lanes, lanes), 1)).astype(BF)
    carry = jnp.zeros((owners, 1), F32)
    counts = []
    for blk in range(blocks):
        local = dot(hot16[:, blk * lanes : (blk + 1) * lanes], upper)
        counts.append(local + carry)
        carry = carry + local[:, lanes - 1 : lanes]
    count = jnp.concatenate(counts, axis=1)
    rank = jnp.sum(count * hot, axis=0, keepdims=True).astype(I32) - 1
    place_ref[...] = tile * slots + rank
    shift = (me_ref[0] % (lanes // slots)) * slots
    load_cell.wait()
    cell = cell_ref[...]
    at = (iota((lanes, records), 0) == rank + shift).astype(BF)
    high = (hot * (cell // lanes + 1).astype(F32)).astype(BF)
    low = (hot * (cell % lanes).astype(F32)).astype(BF)
    high = dot(high, at, 1, 1)
    low = dot(low, at, 1, 1)
    zero = jnp.zeros((6, lanes), F32)
    for t in range(owners):
        extra = jnp.concatenate([high[t : t + 1], low[t : t + 1], zero], axis=0)
        send_ref[t, slots:, :] = extra.astype(BF)
    ranked = (iota((slots, records), 0) == rank).astype(BF)
    group = 512 // slots
    load_feat.wait()
    feat = feat_ref[...]
    for g in range(owners // group):
        for t in range(group):
            mask_ref[t * slots : (t + 1) * slots, :] = ranked * hot16[g * group + t : g * group + t + 1, :]
        rows = dot(mask_ref[...], feat).astype(BF)
        for t in range(group):
            send_ref[g * group + t, :slots, :] = rows[t * slots : (t + 1) * slots]


def unroute_body(place_ref, back_ref, out_ref):
    records = place_ref.shape[1]
    count = back_ref.shape[0]
    size = 512
    place = place_ref[...].astype(F32)
    place = jnp.concatenate([place[:, i : i + 128] for i in range(0, records, 128)], axis=0)
    place = place.T.astype(I32)
    for blk in range(records // size):
        at = jnp.concatenate([place[:, blk * 4 + q : blk * 4 + q + 1] for q in range(4)], axis=0)
        mask = (iota((size, count), 1) == at).astype(BF)
        out_ref[blk * size : (blk + 1) * size, :] = dot(mask, back_ref[...]).astype(BF)


def shifted(row, edge, step):
    cols = row.shape[0]
    wide = pltpu.roll(row.astype(F32), step % cols, 0)
    at = 0 if step == 1 else cols - 1
    return jnp.where(iota((cols, 1), 0) == at, edge.astype(F32), wide).astype(BF)


def conv_body(inside_ref, grid_hbm, left_ref, right_ref, top_ref, bottom_ref, w_hbm, *refs, back, start, total):
    if back:
        out_hbm, pad_hbm, grid_ref, w_ref, pad_ref, out_ref, left32, right32, in_sem, w_sem, out_sem, pad_sem = refs
    else:
        out_hbm, grid_ref, pad_ref, out_ref, left32, right32, in_sem, out_sem = refs[-8:]
        w_ref = w_hbm
    rows, cols, width = out_ref.shape
    held = grid_ref.shape[0]
    base = max(start - 1, 0)
    high = 8
    blocks = rows // high
    cuts = [*range(0, held - 1, high), held]
    loads = [
        begin(grid_hbm.at[base + i : base + j], grid_ref.at[i:j], in_sem.at[n])
        for n, (i, j) in enumerate(zip(cuts[:-1], cuts[1:]))
    ]
    if back:
        load_w = begin(w_hbm, w_ref, w_sem)
    left32[...] = left_ref[...].astype(F32)
    right32[...] = right_ref[...].astype(F32)

    def put(i, row, left, right):
        pad_ref[0, i] = shifted(row, left, 1)
        pad_ref[1, i] = row
        pad_ref[2, i] = shifted(row, right, -1)

    ends = []
    if start == 0:
        ends.append((0, 0, top_ref))
    if start + rows == total:
        ends.append((1, rows + 1, bottom_ref))
    for side, i, ref in ends:

        @pl.when(inside_ref[side] > 0)
        def _():
            put(i, ref[0:cols, :], ref[cols : cols + 1, :], ref[cols + 8 : cols + 9, :])

        @pl.when(inside_ref[side] == 0)
        def _():
            for b in range(3):
                pad_ref[b, i] = jnp.zeros(pad_ref.shape[2:], BF)

    def fill(i, carry):
        at = pl.ds(base + i, 1)
        put(base + i + 1 - start, grid_ref[i], left32[at, :], right32[at, :])
        return carry

    for load, i, j in zip(loads, cuts[:-1], cuts[1:]):
        load.wait()
        lax.fori_loop(i, j, fill, 0)
    stores = []
    if back:
        stores += [begin(pad_ref.at[b], pad_hbm.at[b], pad_sem.at[b]) for b in range(3)]
        load_w.wait()

    def store(n):
        return pltpu.make_async_copy(
            out_ref.at[pl.ds(n * high, high)], out_hbm.at[pl.ds(start + n * high, high)], out_sem.at[n]
        )

    def step(n, carry):
        i = n * high
        acc = grid_ref[pl.ds(start - base + i, high)].astype(F32).reshape(high * cols, width)
        for a in range(3):
            for b in range(3):
                part = pad_ref[b, pl.ds(i + a, high)].reshape(high * cols, width)
                tap = a * 3 + b
                acc = acc + (dot(part, w_ref[8 - tap], 1, 1) if back else dot(part, w_ref[tap]))
        out_ref[pl.ds(i, high)] = acc.astype(BF).reshape(high, cols, width)
        store(n).start()
        return carry

    lax.fori_loop(0, blocks, step, 0)
    for n in range(blocks):
        store(n).wait()
    for move in stores:
        move.wait()


def side_edges(last, first):
    count = lax.axis_size("lon")
    up = [(i, (i + 1) % count) for i in range(count)]
    down = [(j, i) for i, j in up]
    return lax.ppermute(last, "lon", up), lax.ppermute(first, "lon", down)


def end_rows(grid, left, right):
    pad = ((0, 7), (0, 0))

    def row(i):
        return jnp.concatenate([grid[i], jnp.pad(left[i][None], pad), jnp.pad(right[i][None], pad)], axis=0)

    return row(grid.shape[0] - 1), row(0)


def end_edges(last, first):
    count = lax.axis_size("lat")
    up = [(i, (i + 1) % count) for i in range(count)]
    down = [(j, i) for i, j in up]
    return lax.ppermute(last, "lat", up), lax.ppermute(first, "lat", down)


def conv(grid, halo, w, back, start=0, stop=None, into=None):
    total, cols, width = grid.shape
    stop = stop or total
    rows = stop - start
    held = min(stop + 1, total) - max(start - 1, 0)
    outs = [shape(grid.shape, BF)]
    pad = (3, rows + 2, cols, width)
    blocks = rows // 8
    scratch = [
        pltpu.VMEM((held, cols, width), BF),
        pltpu.VMEM(pad, BF),
        pltpu.VMEM((rows, cols, width), BF),
        pltpu.VMEM((total, width), F32),
        pltpu.VMEM((total, width), F32),
        DMA((blocks + 1,)),
        DMA((blocks,)),
    ]
    if back:
        outs.append(shape(pad, BF))
        scratch.insert(1, pltpu.VMEM(w.shape, BF))
        scratch.insert(7, DMA)
        scratch.append(DMA((3,)))
    flops = 18 * rows * cols * width * width
    body = functools.partial(conv_body, back=back, start=start, total=total)
    at = lax.axis_index("lat")
    inside = jnp.stack([at > 0, at < lax.axis_size("lat") - 1]).astype(I32)
    args = [inside, grid, *halo, w]
    alias = {}
    if into is not None:
        alias = {len(args): 0}
        args.append(into)
    return kernel_call(
        body, outs, args, flops, scratch, smem=(0,), hbm=(1, 6 if back else 7), far=(0, 1), temp=8, alias=alias
    )


def gelu_parts(x):
    scale = 0.7978845608028654
    inner = scale * (x + 0.044715 * x * x * x)
    th = jnp.tanh(inner)
    value = 0.5 * x * (1.0 + th)
    slope = 0.5 * (1.0 + th) + 0.5 * x * (1.0 - th * th) * scale * (1.0 + 3 * 0.044715 * x * x)
    return value, slope


def cell_codes(recv_ref, slots):
    owners = recv_ref.shape[0]
    per = 128 // slots
    high, low = [], []
    for p in range(owners // per):
        total = recv_ref[p * per, slots : slots + 8, :].astype(F32)
        for q in range(1, per):
            total = total + recv_ref[p * per + q, slots : slots + 8, :].astype(F32)
        high.append(total[0:1])
        low.append(total[1:2])
    high = jnp.concatenate(high, axis=0)
    low = jnp.concatenate(low, axis=0)
    return (high - 1.0) * 128.0 + low


def gather_body(
    recv_ref, dfield_hbm, w_ref, grad_hbm, eg_hbm, embed_hbm, code_hbm,
    dfield_ref, grad_ref, eg_ref, embed_ref, code_ref, slope_ref, in_sem, grad_sem, out_sem, *, slots,
):
    owners = recv_ref.shape[0]
    cells = dfield_ref.shape[0]
    size = 512
    group = size // slots
    blocks = owners // group
    load = begin(dfield_hbm, dfield_ref, in_sem)
    code_ref[...] = cell_codes(recv_ref, slots)
    stores = [begin(code_ref, code_hbm, out_sem.at[0])]

    def features(blk):
        return jnp.concatenate([recv_ref[blk * group + q, :slots, :] for q in range(group)], axis=0)

    for blk in range(blocks):
        at = slice(blk * size, (blk + 1) * size)
        value, slope = gelu_parts(dot(features(blk), w_ref[...]))
        embed_ref[at, :] = value.astype(BF)
        slope_ref[at, :] = slope
    stores.append(begin(embed_ref, embed_hbm, out_sem.at[1]))
    codes = code_ref[...].T.astype(I32)
    total = jnp.zeros(eg_ref.shape, F32)
    load.wait()
    for blk in range(blocks):
        at = slice(blk * size, (blk + 1) * size)
        code = jnp.concatenate([codes[:, blk * 4 + q : blk * 4 + q + 1] for q in range(4)], axis=0)
        mask = (iota((size, cells), 1) == code).astype(BF)
        rows = dot(mask, dfield_ref[...]).astype(BF)
        grad_ref[at, :] = rows
        stores.append(begin(grad_ref.at[at], grad_hbm.at[at], grad_sem.at[blk]))
        dh = rows.astype(F32) * slope_ref[at, :]
        part = dh.astype(BF)
        rest = (dh - part.astype(F32)).astype(BF)
        feat = features(blk)
        total = total + dot(feat, part, 0, 0) + dot(feat, rest, 0, 0)
    eg_ref[...] = total
    stores.append(begin(eg_ref, eg_hbm, out_sem.at[2]))
    for move in stores:
        move.wait()


def field_body(
    me_ref, code_hbm, embed_hbm, bg_hbm, pad_hbm, eg_hbm, field_hbm, keep_ref, give_ref, last_ref, first_ref,
    code_ref, embed_ref, bg_ref, pad_ref, eg_ref, field_ref, acc_ref, last32, first32, sems, pad_sems, out_sems, bg_sems,
):
    loads = [
        begin(code_hbm, code_ref, sems.at[0]),
        begin(embed_hbm, embed_ref, sems.at[1]),
        begin(pad_hbm.at[:, :2], pad_ref.at[:, :2], sems.at[4]),
    ]
    cells, width = bg_ref.shape
    cols = pad_ref.shape[2]
    half = width // 2
    size = 512
    deep = 2 * size
    high = deep // cols
    blocks = cells // deep

    def load_pad(n):
        some = pl.ds(n * high + 2, high)
        return pltpu.make_async_copy(pad_hbm.at[:, some], pad_ref.at[:, some], pad_sems.at[n])

    def load_bg(n):
        some = pl.ds(pl.multiple_of(n * deep, deep), deep)
        return pltpu.make_async_copy(bg_hbm.at[some], bg_ref.at[some], bg_sems.at[n])

    for n in range(blocks):
        load_bg(n).start()
        load_pad(n).start()
    loads.append(begin(eg_hbm, eg_ref, sems.at[3]))
    acc_ref[...] = jnp.zeros_like(acc_ref)
    for move in loads[:3]:
        move.wait()
    codes = code_ref[...].astype(I32)

    def store(n):
        at = pl.ds(pl.multiple_of(n * deep, deep), deep)
        return pltpu.make_async_copy(field_ref.at[at], field_hbm.at[at], out_sems.at[n])

    def scatter(n):
        for k in range(deep // size):
            base = n * deep + k * size
            where = iota((size, 128), 0) + base
            mask = jnp.concatenate(
                [(where == codes[p : p + 1, :]).astype(BF) for p in range(codes.shape[0])], axis=1
            )
            at = pl.ds(pl.multiple_of(base, size), size)
            total = dot(mask, embed_ref[...]) + bg_ref[at, :].astype(F32)
            field_ref[at, :] = total.astype(BF)
            for g in range(size // cols):
                row = pl.ds(base // cols + g, 1)
                first32[row, :] = total[g * cols : g * cols + 1]
                last32[row, :] = total[(g + 1) * cols - 1 : (g + 1) * cols]
        store(n).start()

    def correlate(n):
        field = field_ref[pl.ds(pl.multiple_of(n * deep, deep), deep), :]
        for a in range(3):
            for b in range(3):
                part = pad_ref[2 - b, pl.ds(n * high + 2 - a, high)].reshape(deep, width)
                acc_ref[3 * a + b] += dot(field, part, 0, 0)

    def step(n, carry):
        load_bg(n).wait()
        scatter(n)
        load_pad(n).wait()
        correlate(n)
        return carry

    lax.fori_loop(0, blocks, step, 0)
    loads[3].wait()
    last_ref[...] = last32[...].astype(BF)
    first_ref[...] = first32[...].astype(BF)
    side = me_ref[0] % 2
    taps = acc_ref.shape[0]
    used = taps * width
    inputs = eg_ref.shape[0]
    for s in range(2):
        lanes = slice(s * half, (s + 1) * half)
        for ref, want in ((keep_ref, s), (give_ref, 1 - s)):

            @pl.when(side == want)
            def _():
                for t in range(taps):
                    ref[t * width : (t + 1) * width, :] = acc_ref[t, :, lanes]
                ref[used : used + inputs, :] = eg_ref[:, lanes]
                if used + inputs < ref.shape[0]:
                    ref[used + inputs :, :] = jnp.zeros((ref.shape[0] - used - inputs, half), F32)

    for n in range(blocks):
        store(n).wait()


def swap(x, bit):
    count = lax.axis_size("lon") * lax.axis_size("lat")
    return lax.ppermute(x, AXES, [(i, i ^ bit) for i in range(count)])


def split_body(mine_ref, *refs, moves, parts):
    n = len(moves)
    ins = refs[: len(refs) - 1 - n]
    keep_ref = refs[len(refs) - 1 - n]
    outs = refs[len(refs) - n :]
    mine = mine_ref[0]

    def put(ref, index):
        row = 0
        for p in range(parts):
            terms = ins[p::parts]
            size = terms[0].shape[0] // (n + 1)
            at = pl.ds(pl.multiple_of(index * size, 8), size)
            total = terms[0][at, :].astype(F32)
            for term in terms[1:]:
                total = total + term[at, :].astype(F32)
            ref[row : row + size, :] = total.astype(ref.dtype)
            row += size

    put(keep_ref, mine)
    for ref, move in zip(outs, moves):
        put(ref, mine ^ move)


def join_body(mine_ref, *refs, parts):
    out_ref = refs[-1]
    ways = len(refs) - 1
    mine = mine_ref[0]
    for move, ref in enumerate(refs[:-1]):
        row, base = 0, 0
        for size in parts:
            at = pl.ds(pl.multiple_of(base + (mine ^ move) * size, 8), size)
            out_ref[at, :] = ref[row : row + size, :]
            row += size
            base += size * ways


def final_body(mine_ref, own_ref, other_ref, conv_ref, embed_ref):
    side = mine_ref[0]
    half = own_ref.shape[1]
    taps, width, _ = conv_ref.shape
    inputs = embed_ref.shape[0]
    for s in range(2):
        lanes = slice(s * half, (s + 1) * half)
        for ref, want in ((own_ref, s), (other_ref, 1 - s)):

            @pl.when(side == want)
            def _():
                for t in range(taps):
                    conv_ref[t, :, lanes] = ref[t * width : (t + 1) * width, :].astype(F32)
                embed_ref[:, lanes] = ref[taps * width : taps * width + inputs, :].astype(F32)


def stages(count):
    bits, found = [], 2
    while found < count:
        bits.append(found)
        found *= 2
    return [bits[i : i + 2] for i in range(0, len(bits), 2)]


def reduce_all(me, keeps, gives, taps, width, inputs, beside, halo_of, encode, unroute):
    count = lax.axis_size("lon") * lax.axis_size("lat")
    terms = [*keeps, *(swap(x, 1) for x in gives)]
    half = width // 2
    plan = stages(count)
    sizes = []
    for bits in plan:
        ways = 2 ** len(bits)
        parts = len(keeps) if bits is plan[0] else 1
        sizes.append([x.shape[0] // ways for x in terms[:parts]])
        mine = (me // bits[0]) % ways
        moves = list(range(1, ways))
        outs = [shape((sum(sizes[-1]), half), F32)] + [shape((sum(sizes[-1]), half), BF)] * len(moves)
        body = functools.partial(split_body, moves=moves, parts=parts)
        own, *send = kernel_call(body, outs, (mine, *terms), smem=(0,))
        if bits is plan[0]:
            send, edges = lax.optimization_barrier((send, beside[1]))
            halo = halo_of(edges)
        terms = [own] + [swap(x, m * bits[0]) for m, x in zip(moves, send)]
        if bits is plan[0]:
            terms, back = lax.optimization_barrier((terms, beside[0]))
        if bits is plan[-1]:
            terms, gone = lax.optimization_barrier((terms, unroute(back)))
    body = functools.partial(split_body, moves=[], parts=1)
    (block,) = kernel_call(
        body, [shape(terms[0].shape, BF)], (jnp.zeros((1,), I32), *terms), smem=(0,)
    )
    for bits, parts in zip(reversed(plan), reversed(sizes)):
        ways = 2 ** len(bits)
        mine = (me // bits[0]) % ways
        pieces = [block] + [swap(block, m * bits[0]) for m in range(1, ways)]
        if bits is plan[-1]:
            pieces, found = lax.optimization_barrier((pieces, encode(halo, 0, None)))
        if bits is plan[0]:
            pieces, found = lax.optimization_barrier((pieces, encode(halo, 1, found)))
        rows = block.shape[0]
        body = functools.partial(join_body, parts=parts)
        (block,) = kernel_call(body, [shape((rows * ways, half), BF)], (mine, *pieces), smem=(0,))
    other = swap(block, 1)
    outs = [shape((taps, width, width), F32), shape((inputs, width), F32)]
    return kernel_call(final_body, outs, (me % 2, block, other), smem=(0,)), found, gone


def on_device(obs_feat, obs_tile, obs_cell, w_embed, background, w_conv, cotangent):
    lon_count = lax.axis_size("lon")
    lat_count = lax.axis_size("lat")
    owners = lon_count * lat_count
    records, inputs = obs_feat.shape
    slots = 2 * records // owners
    rows, cols, width = background.shape
    cells = rows * cols
    taps = w_conv.shape[0]
    me = (lax.axis_index("lon") * lat_count + lax.axis_index("lat")).astype(I32).reshape(1)

    outs = [shape((owners, slots + 8, inputs), BF), shape((1, records), I32)]
    send, place = kernel_call(
        functools.partial(route_body, owners=owners, slots=slots),
        outs,
        (me, obs_tile.reshape(1, records), obs_cell.reshape(1, records), obs_feat),
        flops=4 * records * records * inputs,
        scratch=[
            pltpu.VMEM((512, records), BF),
            pltpu.VMEM((1, records), I32),
            pltpu.VMEM((1, records), I32),
            pltpu.VMEM((records, inputs), BF),
            DMA((3,)),
        ],
        smem=(0,),
        hbm=(1, 2, 3),
        temp=4,
    )
    sides = side_edges(cotangent[:, cols - 1], cotangent[:, 0])
    send, sides = lax.optimization_barrier((send, sides))
    ends = end_rows(cotangent, *sides)
    send, ends = lax.optimization_barrier((send, ends))
    halo = (*sides, *end_edges(*ends))
    recv = lax.all_to_all(send, AXES, split_axis=0, concat_axis=0, tiled=True)

    dfield, pad = conv(cotangent, halo, w_conv, True)

    count = owners * slots
    grad, local_eg, embed, codes = kernel_call(
        functools.partial(gather_body, slots=slots),
        [
            shape((count, width), BF),
            shape((inputs, width), F32),
            shape((count, width), BF),
            shape((count // 128, 128), F32),
        ],
        (recv, dfield.reshape(cells, width), w_embed),
        flops=2 * count * cells * width,
        scratch=[
            pltpu.VMEM((cells, width), BF),
            pltpu.VMEM((count, width), BF),
            pltpu.VMEM((inputs, width), F32),
            pltpu.VMEM((count, width), BF),
            pltpu.VMEM((count // 128, 128), F32),
            pltpu.VMEM((count, width), F32),
            DMA,
            DMA((count // 512,)),
            DMA((3,)),
        ],
        hbm=(1,),
        far=(0, 1, 2, 3),
        temp=12,
    )
    blocks = owners // 2
    size = 8 * blocks
    total = -(-(taps * width + inputs) // size) * size
    back = lax.all_to_all(grad.reshape(owners, slots, width), AXES, split_axis=0, concat_axis=0, tiled=True)
    field, keep, give, last, first = kernel_call(
        field_body,
        [shape((cells, width), BF)]
        + [shape((total, width // 2), F32)] * 2
        + [shape((rows, width), BF)] * 2,
        (me, codes, embed, background.reshape(cells, width), pad, local_eg),
        flops=2 * count * cells * width + 18 * cells * width * width,
        scratch=[
            pltpu.VMEM((count // 128, 128), F32),
            pltpu.VMEM((count, width), BF),
            pltpu.VMEM((cells, width), BF),
            pltpu.VMEM(pad.shape, BF),
            pltpu.VMEM((inputs, width), F32),
            pltpu.VMEM((cells, width), BF),
            pltpu.VMEM((taps, width, width), F32),
            pltpu.VMEM((rows, width), F32),
            pltpu.VMEM((rows, width), F32),
            DMA((5,)),
            DMA((cells // 1024,)),
            DMA((cells // 1024,)),
            DMA((cells // 1024,)),
        ],
        smem=(0,),
        hbm=(1, 2, 3, 4, 5),
        far=(0,),
        temp=8,
    )
    grid = field.reshape(rows, cols, width)

    def halo_of(edges):
        sides = side_edges(*edges)
        return (*sides, *end_edges(*end_rows(grid, *sides)))

    def encode(halo, part, into):
        half = rows // 2
        return conv(grid, halo, w_conv, False, part * half, (part + 1) * half, into)[0]

    def unroute(back):
        return kernel_call(
            unroute_body,
            [shape((records, width), BF)],
            (place, back.reshape(count, width)),
            flops=2 * count * records * width,
            temp=4,
        )[0]

    (conv_grad, embed_grad), encoded, record_grad = reduce_all(
        me, (keep,), (give,), taps, width, inputs, (back, (last, first)), halo_of, encode, unroute
    )
    return encoded, record_grad, conv_grad, embed_grad


def solution(mesh):
    placed = (
        P(("lon", "lat"), None),
        P(("lon", "lat"), None),
        P(("lon", "lat")),
        P(),
        P("lat", "lon", None),
        P(),
        P("lat", "lon", None),
    )
    return jax.shard_map(
        on_device,
        mesh=mesh,
        in_specs=placed,
        out_specs=(P("lat", "lon", None), P(("lon", "lat"), None), P(), P()),
        check_vma=False,
    )
```

```python
import functools
import math

import jax
import jax.numpy as jnp
from jax import lax
from jax.experimental import pallas as pl
from jax.experimental.pallas import tpu as pltpu
from jax.sharding import PartitionSpec as P

AXES = ("lon", "lat")
BF = jnp.bfloat16
F32 = jnp.float32
I32 = jnp.int32


def dot(a, b, ca=1, cb=0):
    return lax.dot_general(a, b, (((ca,), (cb,)), ((), ())), preferred_element_type=F32)


def iota(shape, dim):
    return lax.broadcasted_iota(I32, shape, dim)


def kernel_call(body, outs, args, flops=0, scratch=(), smem=(), hbm=(), far=(), temp=2, alias={}):
    spaces = [
        pltpu.SMEM if i in smem else pltpu.HBM if i in hbm else pltpu.VMEM for i in range(len(args))
    ]
    near = [a for i, a in enumerate(args) if i not in hbm]
    near += [o for i, o in enumerate(outs) if i not in far]
    near += [r for r in scratch if getattr(r, "memory_space", None) == pltpu.VMEM]
    held = sum(math.prod(r.shape) * r.dtype.itemsize for r in near)
    moved = sum(math.prod(r.shape) * r.dtype.itemsize for r in (*args, *outs))
    limit = (held // (1 << 20) + 1 + temp) << 20
    return pl.pallas_call(
        body,
        out_shape=[pltpu.HBM(o.shape, o.dtype) if i in far else o for i, o in enumerate(outs)],
        in_specs=[pl.BlockSpec(memory_space=s) for s in spaces],
        out_specs=[
            pl.BlockSpec(memory_space=pltpu.HBM if i in far else pltpu.VMEM) for i in range(len(outs))
        ],
        scratch_shapes=list(scratch),
        input_output_aliases=alias,
        compiler_params=pltpu.CompilerParams(vmem_limit_bytes=limit),
        cost_estimate=pl.CostEstimate(flops=flops, bytes_accessed=moved, transcendentals=0),
    )(*[pltpu.with_memory_space_constraint(a, pltpu.HBM) if i in hbm else a for i, a in enumerate(args)])


def begin(src, dst, sem):
    move = pltpu.make_async_copy(src, dst, sem)
    move.start()
    return move


DMA = pltpu.SemaphoreType.DMA


def shape(dims, dtype):
    return jax.ShapeDtypeStruct(tuple(dims), dtype)


def route_body(
    me_ref, tile_hbm, cell_hbm, feat_hbm, send_ref, place_ref,
    mask_ref, tile_ref, cell_ref, feat_ref, sems, *, owners, slots,
):
    load_tile = begin(tile_hbm, tile_ref, sems.at[0])
    load_cell = begin(cell_hbm, cell_ref, sems.at[1])
    load_feat = begin(feat_hbm, feat_ref, sems.at[2])
    load_tile.wait()
    records = feat_ref.shape[0]
    lanes = 128
    blocks = records // lanes
    tile = tile_ref[...]
    hot = (iota((owners, records), 0) == tile).astype(F32)
    hot16 = hot.astype(BF)
    upper = (iota((lanes, lanes), 0) <= iota((lanes, lanes), 1)).astype(BF)
    carry = jnp.zeros((owners, 1), F32)
    counts = []
    for blk in range(blocks):
        local = dot(hot16[:, blk * lanes : (blk + 1) * lanes], upper)
        counts.append(local + carry)
        carry = carry + local[:, lanes - 1 : lanes]
    count = jnp.concatenate(counts, axis=1)
    rank = jnp.sum(count * hot, axis=0, keepdims=True).astype(I32) - 1
    place_ref[...] = tile * slots + rank
    shift = (me_ref[0] % (lanes // slots)) * slots
    load_cell.wait()
    cell = cell_ref[...]
    at = (iota((lanes, records), 0) == rank + shift).astype(BF)
    high = (hot * (cell // lanes + 1).astype(F32)).astype(BF)
    low = (hot * (cell % lanes).astype(F32)).astype(BF)
    high = dot(high, at, 1, 1)
    low = dot(low, at, 1, 1)
    zero = jnp.zeros((6, lanes), F32)
    for t in range(owners):
        extra = jnp.concatenate([high[t : t + 1], low[t : t + 1], zero], axis=0)
        send_ref[t, slots:, :] = extra.astype(BF)
    ranked = (iota((slots, records), 0) == rank).astype(BF)
    group = 512 // slots
    load_feat.wait()
    feat = feat_ref[...]
    for g in range(owners // group):
        for t in range(group):
            mask_ref[t * slots : (t + 1) * slots, :] = ranked * hot16[g * group + t : g * group + t + 1, :]
        rows = dot(mask_ref[...], feat).astype(BF)
        for t in range(group):
            send_ref[g * group + t, :slots, :] = rows[t * slots : (t + 1) * slots]


def unroute_body(place_ref, back_ref, out_ref):
    records = place_ref.shape[1]
    count = back_ref.shape[0]
    size = 512
    place = place_ref[...].astype(F32)
    place = jnp.concatenate([place[:, i : i + 128] for i in range(0, records, 128)], axis=0)
    place = place.T.astype(I32)
    for blk in range(records // size):
        at = jnp.concatenate([place[:, blk * 4 + q : blk * 4 + q + 1] for q in range(4)], axis=0)
        mask = (iota((size, count), 1) == at).astype(BF)
        out_ref[blk * size : (blk + 1) * size, :] = dot(mask, back_ref[...]).astype(BF)


def shifted(row, edge, step):
    cols = row.shape[0]
    wide = pltpu.roll(row.astype(F32), step % cols, 0)
    at = 0 if step == 1 else cols - 1
    return jnp.where(iota((cols, 1), 0) == at, edge.astype(F32), wide).astype(BF)


def conv_body(inside_ref, grid_hbm, left_ref, right_ref, top_ref, bottom_ref, w_hbm, *refs, back, start, total):
    if back:
        out_hbm, pad_hbm, grid_ref, w_ref, pad_ref, out_ref, left32, right32, in_sem, w_sem, out_sem, pad_sem = refs
    else:
        out_hbm, pad_ref, out_ref, left32, right32, out_sem = refs[-6:]
        w_ref = w_hbm
    rows, cols, width = out_ref.shape
    base = max(start - 1, 0)
    held = min(start + rows + 1, total) - base
    if not back:
        grid_ref = grid_hbm.at[base : base + held]
    high = 8
    blocks = rows // high
    cuts = [*range(0, held - 1, high), held]
    loads = []
    if back:
        loads = [
            begin(grid_hbm.at[base + i : base + j], grid_ref.at[i:j], in_sem.at[n])
            for n, (i, j) in enumerate(zip(cuts[:-1], cuts[1:]))
        ]
        load_w = begin(w_hbm, w_ref, w_sem)
    left32[...] = left_ref[...].astype(F32)
    right32[...] = right_ref[...].astype(F32)

    def put(i, row, left, right):
        pad_ref[0, i] = shifted(row, left, 1)
        pad_ref[1, i] = row
        pad_ref[2, i] = shifted(row, right, -1)

    ends = []
    if start == 0:
        ends.append((0, 0, top_ref))
    if start + rows == total:
        ends.append((1, rows + 1, bottom_ref))
    for side, i, ref in ends:

        @pl.when(inside_ref[side] > 0)
        def _():
            put(i, ref[0:cols, :], ref[cols : cols + 1, :], ref[cols + 8 : cols + 9, :])

        @pl.when(inside_ref[side] == 0)
        def _():
            for b in range(3):
                pad_ref[b, i] = jnp.zeros(pad_ref.shape[2:], BF)

    def fill(i, carry):
        at = pl.ds(base + i, 1)
        put(base + i + 1 - start, grid_ref[i], left32[at, :], right32[at, :])
        return carry

    for load, i, j in zip(loads, cuts[:-1], cuts[1:]):
        load.wait()
        lax.fori_loop(i, j, fill, 0)
    if not back:
        lax.fori_loop(0, held, fill, 0)
    stores = []
    if back:
        stores += [begin(pad_ref.at[b], pad_hbm.at[b], pad_sem.at[b]) for b in range(3)]
        load_w.wait()

    def store(n):
        return pltpu.make_async_copy(
            out_ref.at[pl.ds(n * high, high)], out_hbm.at[pl.ds(start + n * high, high)], out_sem.at[n]
        )

    def step(n, carry):
        i = n * high
        acc = grid_ref[pl.ds(start - base + i, high)].astype(F32).reshape(high * cols, width)
        for a in range(3):
            for b in range(3):
                part = pad_ref[b, pl.ds(i + a, high)].reshape(high * cols, width)
                tap = a * 3 + b
                acc = acc + (dot(part, w_ref[8 - tap], 1, 1) if back else dot(part, w_ref[tap]))
        out_ref[pl.ds(i, high)] = acc.astype(BF).reshape(high, cols, width)
        store(n).start()
        return carry

    lax.fori_loop(0, blocks, step, 0)
    for n in range(blocks):
        store(n).wait()
    for move in stores:
        move.wait()


def side_edges(last, first):
    count = lax.axis_size("lon")
    up = [(i, (i + 1) % count) for i in range(count)]
    down = [(j, i) for i, j in up]
    return lax.ppermute(last, "lon", up), lax.ppermute(first, "lon", down)


def end_rows(grid, left, right):
    pad = ((0, 7), (0, 0))

    def row(i):
        return jnp.concatenate([grid[i], jnp.pad(left[i][None], pad), jnp.pad(right[i][None], pad)], axis=0)

    return row(grid.shape[0] - 1), row(0)


def end_edges(last, first):
    count = lax.axis_size("lat")
    up = [(i, (i + 1) % count) for i in range(count)]
    down = [(j, i) for i, j in up]
    return lax.ppermute(last, "lat", up), lax.ppermute(first, "lat", down)


def conv(grid, halo, w, back, start=0, stop=None, into=None):
    total, cols, width = grid.shape
    stop = stop or total
    rows = stop - start
    held = min(stop + 1, total) - max(start - 1, 0)
    outs = [shape(grid.shape, BF)]
    pad = (3, rows + 2, cols, width)
    blocks = rows // 8
    scratch = [
        pltpu.VMEM(pad, BF),
        pltpu.VMEM((rows, cols, width), BF),
        pltpu.VMEM((total, width), F32),
        pltpu.VMEM((total, width), F32),
        DMA((blocks,)),
    ]
    if back:
        outs.append(shape(pad, BF))
        scratch = [
            pltpu.VMEM((held, cols, width), BF),
            pltpu.VMEM(w.shape, BF),
            *scratch[:4],
            DMA((blocks + 1,)),
            DMA,
            DMA((blocks,)),
            DMA((3,)),
        ]
    flops = 18 * rows * cols * width * width
    body = functools.partial(conv_body, back=back, start=start, total=total)
    at = lax.axis_index("lat")
    inside = jnp.stack([at > 0, at < lax.axis_size("lat") - 1]).astype(I32)
    args = [inside, grid, *halo, w]
    alias = {}
    if into is not None:
        alias = {len(args): 0}
        args.append(into)
    return kernel_call(
        body, outs, args, flops, scratch, smem=(0,), hbm=(1, 6) if back else (7,), far=(0, 1), temp=8, alias=alias
    )


def gelu_parts(x):
    scale = 0.7978845608028654
    inner = scale * (x + 0.044715 * x * x * x)
    th = jnp.tanh(inner)
    value = 0.5 * x * (1.0 + th)
    slope = 0.5 * (1.0 + th) + 0.5 * x * (1.0 - th * th) * scale * (1.0 + 3 * 0.044715 * x * x)
    return value, slope


def cell_codes(recv_ref, slots):
    owners = recv_ref.shape[0]
    per = 128 // slots
    high, low = [], []
    for p in range(owners // per):
        total = recv_ref[p * per, slots : slots + 8, :].astype(F32)
        for q in range(1, per):
            total = total + recv_ref[p * per + q, slots : slots + 8, :].astype(F32)
        high.append(total[0:1])
        low.append(total[1:2])
    high = jnp.concatenate(high, axis=0)
    low = jnp.concatenate(low, axis=0)
    return (high - 1.0) * 128.0 + low


def gather_body(
    recv_ref, dfield_hbm, w_ref, grad_hbm, eg_hbm, embed_hbm, code_hbm,
    dfield_ref, grad_ref, eg_ref, embed_ref, code_ref, column_ref, slope_ref, in_sem, grad_sem, out_sem, *, slots,
):
    owners = recv_ref.shape[0]
    cells = dfield_ref.shape[0]
    size = 512
    group = size // slots
    blocks = owners // group
    load = begin(dfield_hbm, dfield_ref, in_sem)
    code_ref[...] = cell_codes(recv_ref, slots)
    stores = [begin(code_ref, code_hbm, out_sem.at[0])]

    def features(blk):
        return jnp.concatenate([recv_ref[blk * group + q, :slots, :] for q in range(group)], axis=0)

    codes = code_ref[...].T.astype(I32)
    for p in range(codes.shape[1]):
        column_ref[p * 128 : (p + 1) * 128, :] = codes[:, p : p + 1]

    def activate(blk, carry):
        at = pl.ds(pl.multiple_of(blk * size, size), size)
        value, slope = gelu_parts(dot(features(blk), w_ref[...]))
        embed_ref[at, :] = value.astype(BF)
        slope_ref[at, :] = slope
        return carry

    lax.fori_loop(0, blocks, activate, 0)
    stores.append(begin(embed_ref, embed_hbm, out_sem.at[1]))
    eg_ref[...] = jnp.zeros_like(eg_ref)
    load.wait()

    def store(blk):
        at = pl.ds(pl.multiple_of(blk * size, size), size)
        return pltpu.make_async_copy(grad_ref.at[at], grad_hbm.at[at], grad_sem.at[blk])

    def pick(blk, carry):
        at = pl.ds(pl.multiple_of(blk * size, size), size)
        mask = (iota((size, cells), 1) == column_ref[at, :]).astype(BF)
        rows = dot(mask, dfield_ref[...]).astype(BF)
        grad_ref[at, :] = rows
        store(blk).start()
        dh = rows.astype(F32) * slope_ref[at, :]
        part = dh.astype(BF)
        rest = (dh - part.astype(F32)).astype(BF)
        feat = features(blk)
        eg_ref[...] += dot(feat, part, 0, 0) + dot(feat, rest, 0, 0)
        return carry

    lax.fori_loop(0, blocks, pick, 0)
    stores.append(begin(eg_ref, eg_hbm, out_sem.at[2]))
    for blk in range(blocks):
        store(blk).wait()
    for move in stores:
        move.wait()


def field_body(
    me_ref, code_hbm, embed_hbm, bg_hbm, pad_hbm, eg_hbm, field_hbm, keep_ref, give_ref, last_ref, first_ref,
    code_ref, embed_ref, bg_ref, pad_ref, eg_ref, field_ref, acc_ref, last32, first32, sems, pad_sems, out_sems, bg_sems,
):
    loads = [
        begin(code_hbm, code_ref, sems.at[0]),
        begin(embed_hbm, embed_ref, sems.at[1]),
        begin(pad_hbm.at[:, :2], pad_ref.at[:, :2], sems.at[4]),
    ]
    cells, width = bg_ref.shape
    cols = pad_ref.shape[2]
    half = width // 2
    size = 512
    deep = 2 * size
    high = deep // cols
    blocks = cells // deep

    def load_pad(n):
        some = pl.ds(n * high + 2, high)
        return pltpu.make_async_copy(pad_hbm.at[:, some], pad_ref.at[:, some], pad_sems.at[n])

    def load_bg(n):
        some = pl.ds(pl.multiple_of(n * deep, deep), deep)
        return pltpu.make_async_copy(bg_hbm.at[some], bg_ref.at[some], bg_sems.at[n])

    for n in range(blocks):
        load_bg(n).start()
        load_pad(n).start()
    loads.append(begin(eg_hbm, eg_ref, sems.at[3]))
    acc_ref[...] = jnp.zeros_like(acc_ref)
    for move in loads[:3]:
        move.wait()
    codes = code_ref[...].astype(I32)

    def store(n):
        at = pl.ds(pl.multiple_of(n * deep, deep), deep)
        return pltpu.make_async_copy(field_ref.at[at], field_hbm.at[at], out_sems.at[n])

    def scatter(n):
        for k in range(deep // size):
            base = n * deep + k * size
            where = iota((size, 128), 0) + base
            mask = jnp.concatenate(
                [(where == codes[p : p + 1, :]).astype(BF) for p in range(codes.shape[0])], axis=1
            )
            at = pl.ds(pl.multiple_of(base, size), size)
            total = dot(mask, embed_ref[...]) + bg_ref[at, :].astype(F32)
            field_ref[at, :] = total.astype(BF)
            for g in range(size // cols):
                row = pl.ds(base // cols + g, 1)
                first32[row, :] = total[g * cols : g * cols + 1]
                last32[row, :] = total[(g + 1) * cols - 1 : (g + 1) * cols]
        store(n).start()

    def correlate(n):
        field = field_ref[pl.ds(pl.multiple_of(n * deep, deep), deep), :]
        for a in range(3):
            for b in range(3):
                part = pad_ref[2 - b, pl.ds(n * high + 2 - a, high)].reshape(deep, width)
                acc_ref[3 * a + b] += dot(field, part, 0, 0)

    def step(n, carry):
        load_bg(n).wait()
        scatter(n)
        load_pad(n).wait()
        correlate(n)
        return carry

    lax.fori_loop(0, blocks, step, 0)
    loads[3].wait()
    last_ref[...] = last32[...].astype(BF)
    first_ref[...] = first32[...].astype(BF)
    side = me_ref[0] % 2
    taps = acc_ref.shape[0]
    used = taps * width
    inputs = eg_ref.shape[0]
    for s in range(2):
        lanes = slice(s * half, (s + 1) * half)
        for ref, want in ((keep_ref, s), (give_ref, 1 - s)):

            @pl.when(side == want)
            def _():
                for t in range(taps):
                    ref[t * width : (t + 1) * width, :] = acc_ref[t, :, lanes]
                ref[used : used + inputs, :] = eg_ref[:, lanes]
                if used + inputs < ref.shape[0]:
                    ref[used + inputs :, :] = jnp.zeros((ref.shape[0] - used - inputs, half), F32)

    for n in range(blocks):
        store(n).wait()


def swap(x, bit):
    count = lax.axis_size("lon") * lax.axis_size("lat")
    return lax.ppermute(x, AXES, [(i, i ^ bit) for i in range(count)])


def split_body(mine_ref, *refs, moves, parts):
    n = len(moves)
    ins = refs[: len(refs) - 1 - n]
    keep_ref = refs[len(refs) - 1 - n]
    outs = refs[len(refs) - n :]
    mine = mine_ref[0]

    def put(ref, index):
        row = 0
        for p in range(parts):
            terms = ins[p::parts]
            size = terms[0].shape[0] // (n + 1)
            at = pl.ds(pl.multiple_of(index * size, 8), size)
            total = terms[0][at, :].astype(F32)
            for term in terms[1:]:
                total = total + term[at, :].astype(F32)
            ref[row : row + size, :] = total.astype(ref.dtype)
            row += size

    put(keep_ref, mine)
    for ref, move in zip(outs, moves):
        put(ref, mine ^ move)


def join_body(mine_ref, *refs, parts):
    out_ref = refs[-1]
    ways = len(refs) - 1
    mine = mine_ref[0]
    for move, ref in enumerate(refs[:-1]):
        row, base = 0, 0
        for size in parts:
            at = pl.ds(pl.multiple_of(base + (mine ^ move) * size, 8), size)
            out_ref[at, :] = ref[row : row + size, :]
            row += size
            base += size * ways


def final_body(mine_ref, own_ref, other_ref, conv_ref, embed_ref):
    side = mine_ref[0]
    half = own_ref.shape[1]
    taps, width, _ = conv_ref.shape
    inputs = embed_ref.shape[0]
    for s in range(2):
        lanes = slice(s * half, (s + 1) * half)
        for ref, want in ((own_ref, s), (other_ref, 1 - s)):

            @pl.when(side == want)
            def _():
                for t in range(taps):
                    conv_ref[t, :, lanes] = ref[t * width : (t + 1) * width, :].astype(F32)
                embed_ref[:, lanes] = ref[taps * width : taps * width + inputs, :].astype(F32)


def stages(count):
    bits, found = [], 2
    while found < count:
        bits.append(found)
        found *= 2
    return [bits[i : i + 2] for i in range(0, len(bits), 2)]


def reduce_all(me, keeps, gives, taps, width, inputs, beside, halo_of, encode, unroute):
    count = lax.axis_size("lon") * lax.axis_size("lat")
    terms = [*keeps, *(swap(x, 1) for x in gives)]
    half = width // 2
    plan = stages(count)
    sizes = []
    for bits in plan:
        ways = 2 ** len(bits)
        parts = len(keeps) if bits is plan[0] else 1
        sizes.append([x.shape[0] // ways for x in terms[:parts]])
        mine = (me // bits[0]) % ways
        moves = list(range(1, ways))
        outs = [shape((sum(sizes[-1]), half), F32)] + [shape((sum(sizes[-1]), half), BF)] * len(moves)
        body = functools.partial(split_body, moves=moves, parts=parts)
        own, *send = kernel_call(body, outs, (mine, *terms), smem=(0,))
        if bits is plan[0]:
            send, edges = lax.optimization_barrier((send, beside[1]))
            halo = halo_of(edges)
        terms = [own] + [swap(x, m * bits[0]) for m, x in zip(moves, send)]
        if bits is plan[0]:
            terms, gone = lax.optimization_barrier((terms, unroute(beside[0])))
        if bits is plan[-1]:
            terms, found = lax.optimization_barrier((terms, encode(halo, 0, None)))
    body = functools.partial(split_body, moves=[], parts=1)
    (block,) = kernel_call(
        body, [shape(terms[0].shape, BF)], (jnp.zeros((1,), I32), *terms), smem=(0,)
    )
    for bits, parts in zip(reversed(plan), reversed(sizes)):
        ways = 2 ** len(bits)
        mine = (me // bits[0]) % ways
        pieces = [block] + [swap(block, m * bits[0]) for m in range(1, ways)]
        if bits is plan[-1]:
            pieces, found = lax.optimization_barrier((pieces, encode(halo, 1, found)))
        if bits is plan[0]:
            pieces, found = lax.optimization_barrier((pieces, encode(halo, 2, found)))
        rows = block.shape[0]
        body = functools.partial(join_body, parts=parts)
        (block,) = kernel_call(body, [shape((rows * ways, half), BF)], (mine, *pieces), smem=(0,))
    other = swap(block, 1)
    outs = [shape((taps, width, width), F32), shape((inputs, width), F32)]
    return kernel_call(final_body, outs, (me % 2, block, other), smem=(0,)), found, gone


def on_device(obs_feat, obs_tile, obs_cell, w_embed, background, w_conv, cotangent):
    lon_count = lax.axis_size("lon")
    lat_count = lax.axis_size("lat")
    owners = lon_count * lat_count
    records, inputs = obs_feat.shape
    slots = 2 * records // owners
    rows, cols, width = background.shape
    cells = rows * cols
    taps = w_conv.shape[0]
    me = (lax.axis_index("lon") * lat_count + lax.axis_index("lat")).astype(I32).reshape(1)

    outs = [shape((owners, slots + 8, inputs), BF), shape((1, records), I32)]
    send, place = kernel_call(
        functools.partial(route_body, owners=owners, slots=slots),
        outs,
        (me, obs_tile.reshape(1, records), obs_cell.reshape(1, records), obs_feat),
        flops=4 * records * records * inputs,
        scratch=[
            pltpu.VMEM((512, records), BF),
            pltpu.VMEM((1, records), I32),
            pltpu.VMEM((1, records), I32),
            pltpu.VMEM((records, inputs), BF),
            DMA((3,)),
        ],
        smem=(0,),
        hbm=(1, 2, 3),
        temp=4,
    )
    sides = side_edges(cotangent[:, cols - 1], cotangent[:, 0])
    send, sides = lax.optimization_barrier((send, sides))
    ends = end_rows(cotangent, *sides)
    send, ends = lax.optimization_barrier((send, ends))
    halo = (*sides, *end_edges(*ends))
    recv = lax.all_to_all(send, AXES, split_axis=0, concat_axis=0, tiled=True)

    dfield, pad = conv(cotangent, halo, w_conv, True)

    count = owners * slots
    grad, local_eg, embed, codes = kernel_call(
        functools.partial(gather_body, slots=slots),
        [
            shape((count, width), BF),
            shape((inputs, width), F32),
            shape((count, width), BF),
            shape((count // 128, 128), F32),
        ],
        (recv, dfield.reshape(cells, width), w_embed),
        flops=2 * count * cells * width,
        scratch=[
            pltpu.VMEM((cells, width), BF),
            pltpu.VMEM((count, width), BF),
            pltpu.VMEM((inputs, width), F32),
            pltpu.VMEM((count, width), BF),
            pltpu.VMEM((count // 128, 128), F32),
            pltpu.VMEM((count, 1), I32),
            pltpu.VMEM((count, width), F32),
            DMA,
            DMA((count // 512,)),
            DMA((3,)),
        ],
        hbm=(1,),
        far=(0, 1, 2, 3),
        temp=12,
    )
    blocks = owners // 2
    size = 8 * blocks
    total = -(-(taps * width + inputs) // size) * size
    back = lax.all_to_all(grad.reshape(owners, slots, width), AXES, split_axis=0, concat_axis=0, tiled=True)
    field, keep, give, last, first = kernel_call(
        field_body,
        [shape((cells, width), BF)]
        + [shape((total, width // 2), F32)] * 2
        + [shape((rows, width), BF)] * 2,
        (me, codes, embed, background.reshape(cells, width), pad, local_eg),
        flops=2 * count * cells * width + 18 * cells * width * width,
        scratch=[
            pltpu.VMEM((count // 128, 128), F32),
            pltpu.VMEM((count, width), BF),
            pltpu.VMEM((cells, width), BF),
            pltpu.VMEM(pad.shape, BF),
            pltpu.VMEM((inputs, width), F32),
            pltpu.VMEM((cells, width), BF),
            pltpu.VMEM((taps, width, width), F32),
            pltpu.VMEM((rows, width), F32),
            pltpu.VMEM((rows, width), F32),
            DMA((5,)),
            DMA((cells // 1024,)),
            DMA((cells // 1024,)),
            DMA((cells // 1024,)),
        ],
        smem=(0,),
        hbm=(1, 2, 3, 4, 5),
        far=(0,),
        temp=8,
    )
    grid = field.reshape(rows, cols, width)

    def halo_of(edges):
        sides = side_edges(*edges)
        return (*sides, *end_edges(*end_rows(grid, *sides)))

    def encode(halo, part, into):
        cuts = (0, rows // 4, rows // 2, rows)
        return conv(grid, halo, w_conv, False, cuts[part], cuts[part + 1], into)[0]

    def unroute(back):
        return kernel_call(
            unroute_body,
            [shape((records, width), BF)],
            (place, back.reshape(count, width)),
            flops=2 * count * records * width,
            temp=4,
        )[0]

    (conv_grad, embed_grad), encoded, record_grad = reduce_all(
        me, (keep,), (give,), taps, width, inputs, (back, (last, first)), halo_of, encode, unroute
    )
    return encoded, record_grad, conv_grad, embed_grad


def solution(mesh):
    placed = (
        P(("lon", "lat"), None),
        P(("lon", "lat"), None),
        P(("lon", "lat")),
        P(),
        P("lat", "lon", None),
        P(),
        P("lat", "lon", None),
    )
    return jax.shard_map(
        on_device,
        mesh=mesh,
        in_specs=placed,
        out_specs=(P("lat", "lon", None), P(("lon", "lat"), None), P(), P()),
        check_vma=False,
    )
```

```python
import functools
import math

import jax
import jax.numpy as jnp
from jax import lax
from jax.experimental import pallas as pl
from jax.experimental.pallas import tpu as pltpu
from jax.sharding import PartitionSpec as P

AXES = ("lon", "lat")
BF = jnp.bfloat16
F32 = jnp.float32
I32 = jnp.int32


def dot(a, b, ca=1, cb=0):
    return lax.dot_general(a, b, (((ca,), (cb,)), ((), ())), preferred_element_type=F32)


def iota(shape, dim):
    return lax.broadcasted_iota(I32, shape, dim)


def kernel_call(body, outs, args, flops=0, scratch=(), smem=(), hbm=(), far=(), temp=2, alias={}):
    spaces = [
        pltpu.SMEM if i in smem else pltpu.HBM if i in hbm else pltpu.VMEM for i in range(len(args))
    ]
    near = [a for i, a in enumerate(args) if i not in hbm]
    near += [o for i, o in enumerate(outs) if i not in far]
    near += [r for r in scratch if getattr(r, "memory_space", None) == pltpu.VMEM]
    held = sum(math.prod(r.shape) * r.dtype.itemsize for r in near)
    moved = sum(math.prod(r.shape) * r.dtype.itemsize for r in (*args, *outs))
    limit = (held // (1 << 20) + 1 + temp) << 20
    return pl.pallas_call(
        body,
        out_shape=[pltpu.HBM(o.shape, o.dtype) if i in far else o for i, o in enumerate(outs)],
        in_specs=[pl.BlockSpec(memory_space=s) for s in spaces],
        out_specs=[
            pl.BlockSpec(memory_space=pltpu.HBM if i in far else pltpu.VMEM) for i in range(len(outs))
        ],
        scratch_shapes=list(scratch),
        input_output_aliases=alias,
        compiler_params=pltpu.CompilerParams(vmem_limit_bytes=limit),
        cost_estimate=pl.CostEstimate(flops=flops, bytes_accessed=moved, transcendentals=0),
    )(*[pltpu.with_memory_space_constraint(a, pltpu.HBM) if i in hbm else a for i, a in enumerate(args)])


def begin(src, dst, sem):
    move = pltpu.make_async_copy(src, dst, sem)
    move.start()
    return move


DMA = pltpu.SemaphoreType.DMA


def shape(dims, dtype):
    return jax.ShapeDtypeStruct(tuple(dims), dtype)


def route_body(
    me_ref, tile_hbm, cell_hbm, feat_hbm, send_ref, place_ref,
    mask_ref, tile_ref, cell_ref, feat_ref, sems, *, owners, slots,
):
    load_tile = begin(tile_hbm, tile_ref, sems.at[0])
    load_cell = begin(cell_hbm, cell_ref, sems.at[1])
    load_feat = begin(feat_hbm, feat_ref, sems.at[2])
    load_tile.wait()
    records = feat_ref.shape[0]
    lanes = 128
    blocks = records // lanes
    tile = tile_ref[...]
    hot = (iota((owners, records), 0) == tile).astype(F32)
    hot16 = hot.astype(BF)
    upper = (iota((lanes, lanes), 0) <= iota((lanes, lanes), 1)).astype(BF)
    carry = jnp.zeros((owners, 1), F32)
    counts = []
    for blk in range(blocks):
        local = dot(hot16[:, blk * lanes : (blk + 1) * lanes], upper)
        counts.append(local + carry)
        carry = carry + local[:, lanes - 1 : lanes]
    count = jnp.concatenate(counts, axis=1)
    rank = jnp.sum(count * hot, axis=0, keepdims=True).astype(I32) - 1
    place_ref[...] = tile * slots + rank
    shift = (me_ref[0] % (lanes // slots)) * slots
    load_cell.wait()
    cell = cell_ref[...]
    at = (iota((lanes, records), 0) == rank + shift).astype(BF)
    high = (hot * (cell // lanes + 1).astype(F32)).astype(BF)
    low = (hot * (cell % lanes).astype(F32)).astype(BF)
    high = dot(high, at, 1, 1)
    low = dot(low, at, 1, 1)
    zero = jnp.zeros((6, lanes), F32)
    for t in range(owners):
        extra = jnp.concatenate([high[t : t + 1], low[t : t + 1], zero], axis=0)
        send_ref[t, slots:, :] = extra.astype(BF)
    ranked = (iota((slots, records), 0) == rank).astype(BF)
    group = 512 // slots
    load_feat.wait()
    feat = feat_ref[...]
    for g in range(owners // group):
        for t in range(group):
            mask_ref[t * slots : (t + 1) * slots, :] = ranked * hot16[g * group + t : g * group + t + 1, :]
        rows = dot(mask_ref[...], feat).astype(BF)
        for t in range(group):
            send_ref[g * group + t, :slots, :] = rows[t * slots : (t + 1) * slots]


def unroute_body(place_ref, back_ref, out_ref):
    records = place_ref.shape[1]
    count = back_ref.shape[0]
    size = 512
    place = place_ref[...].astype(F32)
    place = jnp.concatenate([place[:, i : i + 128] for i in range(0, records, 128)], axis=0)
    place = place.T.astype(I32)
    for blk in range(records // size):
        at = jnp.concatenate([place[:, blk * 4 + q : blk * 4 + q + 1] for q in range(4)], axis=0)
        mask = (iota((size, count), 1) == at).astype(BF)
        out_ref[blk * size : (blk + 1) * size, :] = dot(mask, back_ref[...]).astype(BF)


def shifted(row, edge, step):
    cols = row.shape[0]
    wide = pltpu.roll(row.astype(F32), step % cols, 0)
    at = 0 if step == 1 else cols - 1
    return jnp.where(iota((cols, 1), 0) == at, edge.astype(F32), wide).astype(BF)


def conv_body(inside_ref, grid_hbm, left_ref, right_ref, top_ref, bottom_ref, w_hbm, *refs, back, start, total):
    if back:
        out_hbm, pad_hbm, grid_ref, w_ref, pad_ref, out_ref, left32, right32, in_sem, w_sem, out_sem, pad_sem = refs
    else:
        out_hbm, pad_ref, out_ref, left32, right32, out_sem = refs[-6:]
        w_ref = w_hbm
    rows, cols, width = out_ref.shape
    base = max(start - 1, 0)
    held = min(start + rows + 1, total) - base
    if not back:
        grid_ref = grid_hbm.at[base : base + held]
    high = 8
    blocks = rows // high
    cuts = [*range(0, held - 1, high), held]
    loads = []
    if back:
        loads = [
            begin(grid_hbm.at[base + i : base + j], grid_ref.at[i:j], in_sem.at[n])
            for n, (i, j) in enumerate(zip(cuts[:-1], cuts[1:]))
        ]
        load_w = begin(w_hbm, w_ref, w_sem)
    left32[...] = left_ref[...].astype(F32)
    right32[...] = right_ref[...].astype(F32)

    def put(i, row, left, right):
        pad_ref[0, i] = shifted(row, left, 1)
        pad_ref[1, i] = row
        pad_ref[2, i] = shifted(row, right, -1)

    ends = []
    if start == 0:
        ends.append((0, 0, top_ref))
    if start + rows == total:
        ends.append((1, rows + 1, bottom_ref))
    for side, i, ref in ends:

        @pl.when(inside_ref[side] > 0)
        def _():
            put(i, ref[0:cols, :], ref[cols : cols + 1, :], ref[cols + 8 : cols + 9, :])

        @pl.when(inside_ref[side] == 0)
        def _():
            for b in range(3):
                pad_ref[b, i] = jnp.zeros(pad_ref.shape[2:], BF)

    def fill(i, carry):
        at = pl.ds(base + i, 1)
        put(base + i + 1 - start, grid_ref[i], left32[at, :], right32[at, :])
        return carry

    for load, i, j in zip(loads, cuts[:-1], cuts[1:]):
        load.wait()
        lax.fori_loop(i, j, fill, 0)
    if not back:
        lax.fori_loop(0, held, fill, 0)
    stores = []
    if back:
        stores += [begin(pad_ref.at[b], pad_hbm.at[b], pad_sem.at[b]) for b in range(3)]
        load_w.wait()

    def store(n):
        return pltpu.make_async_copy(
            out_ref.at[pl.ds(n * high, high)], out_hbm.at[pl.ds(start + n * high, high)], out_sem.at[n]
        )

    def step(n, carry):
        i = n * high
        acc = grid_ref[pl.ds(start - base + i, high)].astype(F32).reshape(high * cols, width)
        for a in range(3):
            for b in range(3):
                part = pad_ref[b, pl.ds(i + a, high)].reshape(high * cols, width)
                tap = a * 3 + b
                acc = acc + (dot(part, w_ref[8 - tap], 1, 1) if back else dot(part, w_ref[tap]))
        out_ref[pl.ds(i, high)] = acc.astype(BF).reshape(high, cols, width)
        store(n).start()
        return carry

    lax.fori_loop(0, blocks, step, 0)
    for n in range(blocks):
        store(n).wait()
    for move in stores:
        move.wait()


def side_edges(last, first):
    count = lax.axis_size("lon")
    up = [(i, (i + 1) % count) for i in range(count)]
    down = [(j, i) for i, j in up]
    return lax.ppermute(last, "lon", up), lax.ppermute(first, "lon", down)


def end_rows(grid, left, right):
    pad = ((0, 7), (0, 0))

    def row(i):
        return jnp.concatenate([grid[i], jnp.pad(left[i][None], pad), jnp.pad(right[i][None], pad)], axis=0)

    return row(grid.shape[0] - 1), row(0)


def end_edges(last, first):
    count = lax.axis_size("lat")
    up = [(i, (i + 1) % count) for i in range(count)]
    down = [(j, i) for i, j in up]
    return lax.ppermute(last, "lat", up), lax.ppermute(first, "lat", down)


def conv(grid, halo, w, back, start=0, stop=None, into=None):
    total, cols, width = grid.shape
    stop = stop or total
    rows = stop - start
    held = min(stop + 1, total) - max(start - 1, 0)
    outs = [shape(grid.shape, BF)]
    pad = (3, rows + 2, cols, width)
    blocks = rows // 8
    scratch = [
        pltpu.VMEM(pad, BF),
        pltpu.VMEM((rows, cols, width), BF),
        pltpu.VMEM((total, width), F32),
        pltpu.VMEM((total, width), F32),
        DMA((blocks,)),
    ]
    if back:
        outs.append(shape(pad, BF))
        scratch = [
            pltpu.VMEM((held, cols, width), BF),
            pltpu.VMEM(w.shape, BF),
            *scratch[:4],
            DMA((blocks + 1,)),
            DMA,
            DMA((blocks,)),
            DMA((3,)),
        ]
    flops = 18 * rows * cols * width * width
    body = functools.partial(conv_body, back=back, start=start, total=total)
    at = lax.axis_index("lat")
    inside = jnp.stack([at > 0, at < lax.axis_size("lat") - 1]).astype(I32)
    args = [inside, grid, *halo, w]
    alias = {}
    if into is not None:
        alias = {len(args): 0}
        args.append(into)
    return kernel_call(
        body, outs, args, flops, scratch, smem=(0,), hbm=(1, 6) if back else (7,), far=(0, 1), temp=8, alias=alias
    )


def gelu_parts(x):
    scale = 0.7978845608028654
    inner = scale * (x + 0.044715 * x * x * x)
    th = jnp.tanh(inner)
    value = 0.5 * x * (1.0 + th)
    slope = 0.5 * (1.0 + th) + 0.5 * x * (1.0 - th * th) * scale * (1.0 + 3 * 0.044715 * x * x)
    return value, slope


def cell_codes(recv_ref, slots):
    owners = recv_ref.shape[0]
    per = 128 // slots
    high, low = [], []
    for p in range(owners // per):
        total = recv_ref[p * per, slots : slots + 8, :].astype(F32)
        for q in range(1, per):
            total = total + recv_ref[p * per + q, slots : slots + 8, :].astype(F32)
        high.append(total[0:1])
        low.append(total[1:2])
    high = jnp.concatenate(high, axis=0)
    low = jnp.concatenate(low, axis=0)
    return (high - 1.0) * 128.0 + low


def gather_body(
    recv_ref, dfield_hbm, w_ref, grad_hbm, eg_hbm, embed_hbm, code_hbm,
    dfield_ref, grad_ref, eg_ref, embed_ref, code_ref, column_ref, slope_ref, in_sem, grad_sem, out_sem, *, slots,
):
    owners = recv_ref.shape[0]
    cells = dfield_ref.shape[0]
    size = 512
    group = size // slots
    blocks = owners // group
    load = begin(dfield_hbm, dfield_ref, in_sem)
    code_ref[...] = cell_codes(recv_ref, slots)
    stores = [begin(code_ref, code_hbm, out_sem.at[0])]

    def features(blk):
        return jnp.concatenate([recv_ref[blk * group + q, :slots, :] for q in range(group)], axis=0)

    codes = code_ref[...].T.astype(I32)
    for p in range(codes.shape[1]):
        column_ref[p * 128 : (p + 1) * 128, :] = codes[:, p : p + 1]

    def activate(blk, carry):
        at = pl.ds(pl.multiple_of(blk * size, size), size)
        value, slope = gelu_parts(dot(features(blk), w_ref[...]))
        embed_ref[at, :] = value.astype(BF)
        slope_ref[at, :] = slope
        return carry

    lax.fori_loop(0, blocks, activate, 0)
    stores.append(begin(embed_ref, embed_hbm, out_sem.at[1]))
    eg_ref[...] = jnp.zeros_like(eg_ref)
    load.wait()

    def store(blk):
        at = pl.ds(pl.multiple_of(blk * size, size), size)
        return pltpu.make_async_copy(grad_ref.at[at], grad_hbm.at[at], grad_sem.at[blk])

    def pick(blk, carry):
        at = pl.ds(pl.multiple_of(blk * size, size), size)
        mask = (iota((size, cells), 1) == column_ref[at, :]).astype(BF)
        rows = dot(mask, dfield_ref[...]).astype(BF)
        grad_ref[at, :] = rows
        store(blk).start()
        dh = rows.astype(F32) * slope_ref[at, :]
        part = dh.astype(BF)
        rest = (dh - part.astype(F32)).astype(BF)
        feat = features(blk)
        eg_ref[...] += dot(feat, part, 0, 0) + dot(feat, rest, 0, 0)
        return carry

    lax.fori_loop(0, blocks, pick, 0)
    stores.append(begin(eg_ref, eg_hbm, out_sem.at[2]))
    for blk in range(blocks):
        store(blk).wait()
    for move in stores:
        move.wait()


def field_body(
    me_ref, code_hbm, embed_hbm, bg_hbm, pad_hbm, eg_hbm, field_hbm, keep_ref, give_ref, last_ref, first_ref,
    code_ref, embed_ref, bg_ref, pad_ref, eg_ref, field_ref, acc_ref, last32, first32, sems, pad_sems, out_sems, bg_sems,
):
    loads = [
        begin(code_hbm, code_ref, sems.at[0]),
        begin(embed_hbm, embed_ref, sems.at[1]),
        begin(pad_hbm.at[:, :2], pad_ref.at[:, :2], sems.at[4]),
    ]
    cells, width = bg_ref.shape
    cols = pad_ref.shape[2]
    half = width // 2
    size = 512
    deep = 2 * size
    high = deep // cols
    blocks = cells // deep

    def load_pad(n):
        some = pl.ds(n * high + 2, high)
        return pltpu.make_async_copy(pad_hbm.at[:, some], pad_ref.at[:, some], pad_sems.at[n])

    def load_bg(n):
        some = pl.ds(pl.multiple_of(n * deep, deep), deep)
        return pltpu.make_async_copy(bg_hbm.at[some], bg_ref.at[some], bg_sems.at[n])

    for n in range(blocks):
        load_bg(n).start()
        load_pad(n).start()
    loads.append(begin(eg_hbm, eg_ref, sems.at[3]))
    acc_ref[...] = jnp.zeros_like(acc_ref)
    for move in loads[:3]:
        move.wait()
    codes = code_ref[...].astype(I32)

    def store(n):
        at = pl.ds(pl.multiple_of(n * deep, deep), deep)
        return pltpu.make_async_copy(field_ref.at[at], field_hbm.at[at], out_sems.at[n])

    def scatter(n):
        for k in range(deep // size):
            base = n * deep + k * size
            where = iota((size, 128), 0) + base
            mask = jnp.concatenate(
                [(where == codes[p : p + 1, :]).astype(BF) for p in range(codes.shape[0])], axis=1
            )
            at = pl.ds(pl.multiple_of(base, size), size)
            total = dot(mask, embed_ref[...]) + bg_ref[at, :].astype(F32)
            field_ref[at, :] = total.astype(BF)
            for g in range(size // cols):
                row = pl.ds(base // cols + g, 1)
                first32[row, :] = total[g * cols : g * cols + 1]
                last32[row, :] = total[(g + 1) * cols - 1 : (g + 1) * cols]
        store(n).start()

    def correlate(n):
        field = field_ref[pl.ds(pl.multiple_of(n * deep, deep), deep), :]
        for a in range(3):
            for b in range(3):
                part = pad_ref[2 - b, pl.ds(n * high + 2 - a, high)].reshape(deep, width)
                acc_ref[3 * a + b] += dot(field, part, 0, 0)

    def step(n, carry):
        load_bg(n).wait()
        scatter(n)
        load_pad(n).wait()
        correlate(n)
        return carry

    lax.fori_loop(0, blocks, step, 0)
    loads[3].wait()
    last_ref[...] = last32[...].astype(BF)
    first_ref[...] = first32[...].astype(BF)
    side = me_ref[0] % 2
    taps = acc_ref.shape[0]
    used = taps * width
    inputs = eg_ref.shape[0]
    for s in range(2):
        lanes = slice(s * half, (s + 1) * half)
        for ref, want in ((keep_ref, s), (give_ref, 1 - s)):

            @pl.when(side == want)
            def _():
                for t in range(taps):
                    ref[t * width : (t + 1) * width, :] = acc_ref[t, :, lanes]
                ref[used : used + inputs, :] = eg_ref[:, lanes]
                if used + inputs < ref.shape[0]:
                    ref[used + inputs :, :] = jnp.zeros((ref.shape[0] - used - inputs, half), F32)

    for n in range(blocks):
        store(n).wait()


def swap(x, bit):
    count = lax.axis_size("lon") * lax.axis_size("lat")
    return lax.ppermute(x, AXES, [(i, i ^ bit) for i in range(count)])


def split_body(mine_ref, *refs, moves, parts):
    n = len(moves)
    ins = refs[: len(refs) - 1 - n]
    keep_ref = refs[len(refs) - 1 - n]
    outs = refs[len(refs) - n :]
    mine = mine_ref[0]

    def put(ref, index):
        row = 0
        for p in range(parts):
            terms = ins[p::parts]
            size = terms[0].shape[0] // (n + 1)
            at = pl.ds(pl.multiple_of(index * size, 8), size)
            total = terms[0][at, :].astype(F32)
            for term in terms[1:]:
                total = total + term[at, :].astype(F32)
            ref[row : row + size, :] = total.astype(ref.dtype)
            row += size

    put(keep_ref, mine)
    for ref, move in zip(outs, moves):
        put(ref, mine ^ move)


def join_body(mine_ref, *refs, parts):
    out_ref = refs[-1]
    ways = len(refs) - 1
    mine = mine_ref[0]
    for move, ref in enumerate(refs[:-1]):
        row, base = 0, 0
        for size in parts:
            at = pl.ds(pl.multiple_of(base + (mine ^ move) * size, 8), size)
            out_ref[at, :] = ref[row : row + size, :]
            row += size
            base += size * ways


def final_body(mine_ref, own_ref, other_ref, conv_ref, embed_ref):
    side = mine_ref[0]
    half = own_ref.shape[1]
    taps, width, _ = conv_ref.shape
    inputs = embed_ref.shape[0]
    for s in range(2):
        lanes = slice(s * half, (s + 1) * half)
        for ref, want in ((own_ref, s), (other_ref, 1 - s)):

            @pl.when(side == want)
            def _():
                for t in range(taps):
                    conv_ref[t, :, lanes] = ref[t * width : (t + 1) * width, :].astype(F32)
                embed_ref[:, lanes] = ref[taps * width : taps * width + inputs, :].astype(F32)


def stages(count):
    bits, found = [], 2
    while found < count:
        bits.append(found)
        found *= 2
    return [bits[i : i + 2] for i in range(0, len(bits), 2)]


def reduce_all(me, keeps, gives, taps, width, inputs, beside, halo_of, encode, unroute):
    count = lax.axis_size("lon") * lax.axis_size("lat")
    terms = [*keeps, *(swap(x, 1) for x in gives)]
    half = width // 2
    plan = stages(count)
    sizes = []
    for bits in plan:
        ways = 2 ** len(bits)
        parts = len(keeps) if bits is plan[0] else 1
        sizes.append([x.shape[0] // ways for x in terms[:parts]])
        mine = (me // bits[0]) % ways
        moves = list(range(1, ways))
        outs = [shape((sum(sizes[-1]), half), F32)] + [shape((sum(sizes[-1]), half), BF)] * len(moves)
        body = functools.partial(split_body, moves=moves, parts=parts)
        own, *send = kernel_call(body, outs, (mine, *terms), smem=(0,))
        if bits is plan[0]:
            send, edges = lax.optimization_barrier((send, beside[1]))
            halo = halo_of(edges)
        terms = [own] + [swap(x, m * bits[0]) for m, x in zip(moves, send)]
        if bits is plan[0]:
            terms, back = lax.optimization_barrier((terms, beside[0]))
        if bits is plan[-1]:
            terms, gone = lax.optimization_barrier((terms, unroute(back)))
    body = functools.partial(split_body, moves=[], parts=1)
    (block,) = kernel_call(
        body, [shape(terms[0].shape, BF)], (jnp.zeros((1,), I32), *terms), smem=(0,)
    )
    for bits, parts in zip(reversed(plan), reversed(sizes)):
        ways = 2 ** len(bits)
        mine = (me // bits[0]) % ways
        pieces = [block] + [swap(block, m * bits[0]) for m in range(1, ways)]
        if bits is plan[-1]:
            pieces, found = lax.optimization_barrier((pieces, encode(halo, 0, None)))
        if bits is plan[0]:
            pieces, found = lax.optimization_barrier((pieces, encode(halo, 1, found)))
        rows = block.shape[0]
        body = functools.partial(join_body, parts=parts)
        (block,) = kernel_call(body, [shape((rows * ways, half), BF)], (mine, *pieces), smem=(0,))
    other = swap(block, 1)
    outs = [shape((taps, width, width), F32), shape((inputs, width), F32)]
    return kernel_call(final_body, outs, (me % 2, block, other), smem=(0,)), found, gone


def on_device(obs_feat, obs_tile, obs_cell, w_embed, background, w_conv, cotangent):
    lon_count = lax.axis_size("lon")
    lat_count = lax.axis_size("lat")
    owners = lon_count * lat_count
    records, inputs = obs_feat.shape
    slots = 2 * records // owners
    rows, cols, width = background.shape
    cells = rows * cols
    taps = w_conv.shape[0]
    me = (lax.axis_index("lon") * lat_count + lax.axis_index("lat")).astype(I32).reshape(1)

    outs = [shape((owners, slots + 8, inputs), BF), shape((1, records), I32)]
    send, place = kernel_call(
        functools.partial(route_body, owners=owners, slots=slots),
        outs,
        (me, obs_tile.reshape(1, records), obs_cell.reshape(1, records), obs_feat),
        flops=4 * records * records * inputs,
        scratch=[
            pltpu.VMEM((512, records), BF),
            pltpu.VMEM((1, records), I32),
            pltpu.VMEM((1, records), I32),
            pltpu.VMEM((records, inputs), BF),
            DMA((3,)),
        ],
        smem=(0,),
        hbm=(1, 2, 3),
        temp=4,
    )
    sides = side_edges(cotangent[:, cols - 1], cotangent[:, 0])
    send, sides = lax.optimization_barrier((send, sides))
    ends = end_rows(cotangent, *sides)
    send, ends = lax.optimization_barrier((send, ends))
    halo = (*sides, *end_edges(*ends))
    recv = lax.all_to_all(send, AXES, split_axis=0, concat_axis=0, tiled=True)

    dfield, pad = conv(cotangent, halo, w_conv, True)

    count = owners * slots
    grad, local_eg, embed, codes = kernel_call(
        functools.partial(gather_body, slots=slots),
        [
            shape((count, width), BF),
            shape((inputs, width), F32),
            shape((count, width), BF),
            shape((count // 128, 128), F32),
        ],
        (recv, dfield.reshape(cells, width), w_embed),
        flops=2 * count * cells * width,
        scratch=[
            pltpu.VMEM((cells, width), BF),
            pltpu.VMEM((count, width), BF),
            pltpu.VMEM((inputs, width), F32),
            pltpu.VMEM((count, width), BF),
            pltpu.VMEM((count // 128, 128), F32),
            pltpu.VMEM((count, 1), I32),
            pltpu.VMEM((count, width), F32),
            DMA,
            DMA((count // 512,)),
            DMA((3,)),
        ],
        hbm=(1,),
        far=(0, 1, 2, 3),
        temp=12,
    )
    blocks = owners // 2
    size = 8 * blocks
    total = -(-(taps * width + inputs) // size) * size
    back = lax.all_to_all(grad.reshape(owners, slots, width), AXES, split_axis=0, concat_axis=0, tiled=True)
    field, keep, give, last, first = kernel_call(
        field_body,
        [shape((cells, width), BF)]
        + [shape((total, width // 2), F32)] * 2
        + [shape((rows, width), BF)] * 2,
        (me, codes, embed, background.reshape(cells, width), pad, local_eg),
        flops=2 * count * cells * width + 18 * cells * width * width,
        scratch=[
            pltpu.VMEM((count // 128, 128), F32),
            pltpu.VMEM((count, width), BF),
            pltpu.VMEM((cells, width), BF),
            pltpu.VMEM(pad.shape, BF),
            pltpu.VMEM((inputs, width), F32),
            pltpu.VMEM((cells, width), BF),
            pltpu.VMEM((taps, width, width), F32),
            pltpu.VMEM((rows, width), F32),
            pltpu.VMEM((rows, width), F32),
            DMA((5,)),
            DMA((cells // 1024,)),
            DMA((cells // 1024,)),
            DMA((cells // 1024,)),
        ],
        smem=(0,),
        hbm=(1, 2, 3, 4, 5),
        far=(0,),
        temp=8,
    )
    grid = field.reshape(rows, cols, width)

    def halo_of(edges):
        sides = side_edges(*edges)
        return (*sides, *end_edges(*end_rows(grid, *sides)))

    def encode(halo, part, into):
        cuts = (0, rows // 2, rows)
        return conv(grid, halo, w_conv, False, cuts[part], cuts[part + 1], into)[0]

    def unroute(back):
        return kernel_call(
            unroute_body,
            [shape((records, width), BF)],
            (place, back.reshape(count, width)),
            flops=2 * count * records * width,
            temp=4,
        )[0]

    (conv_grad, embed_grad), encoded, record_grad = reduce_all(
        me, (keep,), (give,), taps, width, inputs, (back, (last, first)), halo_of, encode, unroute
    )
    return encoded, record_grad, conv_grad, embed_grad


def solution(mesh):
    placed = (
        P(("lon", "lat"), None),
        P(("lon", "lat"), None),
        P(("lon", "lat")),
        P(),
        P("lat", "lon", None),
        P(),
        P("lat", "lon", None),
    )
    return jax.shard_map(
        on_device,
        mesh=mesh,
        in_specs=placed,
        out_specs=(P("lat", "lon", None), P(("lon", "lat"), None), P(), P()),
        check_vma=False,
    )
```

```python
import functools
import math

import jax
import jax.numpy as jnp
from jax import lax
from jax.experimental import pallas as pl
from jax.experimental.pallas import tpu as pltpu
from jax.sharding import PartitionSpec as P

AXES = ("lon", "lat")
BF = jnp.bfloat16
F32 = jnp.float32
I32 = jnp.int32


def dot(a, b, ca=1, cb=0):
    return lax.dot_general(a, b, (((ca,), (cb,)), ((), ())), preferred_element_type=F32)


def iota(shape, dim):
    return lax.broadcasted_iota(I32, shape, dim)


def kernel_call(body, outs, args, flops=0, scratch=(), smem=(), hbm=(), far=(), temp=2, alias={}):
    spaces = [
        pltpu.SMEM if i in smem else pltpu.HBM if i in hbm else pltpu.VMEM for i in range(len(args))
    ]
    near = [a for i, a in enumerate(args) if i not in hbm]
    near += [o for i, o in enumerate(outs) if i not in far]
    near += [r for r in scratch if getattr(r, "memory_space", None) == pltpu.VMEM]
    held = sum(math.prod(r.shape) * r.dtype.itemsize for r in near)
    moved = sum(math.prod(r.shape) * r.dtype.itemsize for r in (*args, *outs))
    limit = (held // (1 << 20) + 1 + temp) << 20
    return pl.pallas_call(
        body,
        out_shape=[pltpu.HBM(o.shape, o.dtype) if i in far else o for i, o in enumerate(outs)],
        in_specs=[pl.BlockSpec(memory_space=s) for s in spaces],
        out_specs=[
            pl.BlockSpec(memory_space=pltpu.HBM if i in far else pltpu.VMEM) for i in range(len(outs))
        ],
        scratch_shapes=list(scratch),
        input_output_aliases=alias,
        compiler_params=pltpu.CompilerParams(vmem_limit_bytes=limit),
        cost_estimate=pl.CostEstimate(flops=flops, bytes_accessed=moved, transcendentals=0),
    )(*[pltpu.with_memory_space_constraint(a, pltpu.HBM) if i in hbm else a for i, a in enumerate(args)])


def begin(src, dst, sem):
    move = pltpu.make_async_copy(src, dst, sem)
    move.start()
    return move


DMA = pltpu.SemaphoreType.DMA


def shape(dims, dtype):
    return jax.ShapeDtypeStruct(tuple(dims), dtype)


def route_body(
    me_ref, tile_hbm, cell_hbm, feat_hbm, send_ref, place_ref,
    mask_ref, tile_ref, cell_ref, feat_ref, sems, *, owners, slots,
):
    load_tile = begin(tile_hbm, tile_ref, sems.at[0])
    load_cell = begin(cell_hbm, cell_ref, sems.at[1])
    load_feat = begin(feat_hbm, feat_ref, sems.at[2])
    load_tile.wait()
    records = feat_ref.shape[0]
    lanes = 128
    blocks = records // lanes
    tile = tile_ref[...]
    hot = (iota((owners, records), 0) == tile).astype(F32)
    hot16 = hot.astype(BF)
    upper = (iota((lanes, lanes), 0) <= iota((lanes, lanes), 1)).astype(BF)
    carry = jnp.zeros((owners, 1), F32)
    counts = []
    for blk in range(blocks):
        local = dot(hot16[:, blk * lanes : (blk + 1) * lanes], upper)
        counts.append(local + carry)
        carry = carry + local[:, lanes - 1 : lanes]
    count = jnp.concatenate(counts, axis=1)
    rank = jnp.sum(count * hot, axis=0, keepdims=True).astype(I32) - 1
    place_ref[...] = tile * slots + rank
    shift = (me_ref[0] % (lanes // slots)) * slots
    load_cell.wait()
    cell = cell_ref[...]
    at = (iota((lanes, records), 0) == rank + shift).astype(BF)
    high = (hot * (cell // lanes + 1).astype(F32)).astype(BF)
    low = (hot * (cell % lanes).astype(F32)).astype(BF)
    high = dot(high, at, 1, 1)
    low = dot(low, at, 1, 1)
    zero = jnp.zeros((6, lanes), F32)
    for t in range(owners):
        extra = jnp.concatenate([high[t : t + 1], low[t : t + 1], zero], axis=0)
        send_ref[t, slots:, :] = extra.astype(BF)
    ranked = (iota((slots, records), 0) == rank).astype(BF)
    group = 512 // slots
    load_feat.wait()
    feat = feat_ref[...]
    for g in range(owners // group):
        for t in range(group):
            mask_ref[t * slots : (t + 1) * slots, :] = ranked * hot16[g * group + t : g * group + t + 1, :]
        rows = dot(mask_ref[...], feat).astype(BF)
        for t in range(group):
            send_ref[g * group + t, :slots, :] = rows[t * slots : (t + 1) * slots]


def unroute_body(place_ref, back_ref, out_ref):
    records = place_ref.shape[1]
    count = back_ref.shape[0]
    size = 512
    place = place_ref[...].astype(F32)
    place = jnp.concatenate([place[:, i : i + 128] for i in range(0, records, 128)], axis=0)
    place = place.T.astype(I32)
    for blk in range(records // size):
        at = jnp.concatenate([place[:, blk * 4 + q : blk * 4 + q + 1] for q in range(4)], axis=0)
        mask = (iota((size, count), 1) == at).astype(BF)
        out_ref[blk * size : (blk + 1) * size, :] = dot(mask, back_ref[...]).astype(BF)


def shifted(row, edge, step):
    cols = row.shape[0]
    wide = pltpu.roll(row.astype(F32), step % cols, 0)
    at = 0 if step == 1 else cols - 1
    return jnp.where(iota((cols, 1), 0) == at, edge.astype(F32), wide).astype(BF)


def conv_body(inside_ref, grid_hbm, left_ref, right_ref, top_ref, bottom_ref, w_hbm, *refs, back, start, total):
    if back:
        out_hbm, pad_hbm, grid_ref, w_ref, pad_ref, out_ref, left32, right32, in_sem, w_sem, out_sem, pad_sem = refs
    else:
        out_hbm, pad_ref, out_ref, left32, right32, out_sem = refs[-6:]
        w_ref = w_hbm
    rows, cols, width = out_ref.shape
    base = max(start - 1, 0)
    held = min(start + rows + 1, total) - base
    if not back:
        grid_ref = grid_hbm.at[base : base + held]
    high = 8
    blocks = rows // high
    cuts = [*range(0, held - 1, high), held]
    loads = []
    if back:
        loads = [
            begin(grid_hbm.at[base + i : base + j], grid_ref.at[i:j], in_sem.at[n])
            for n, (i, j) in enumerate(zip(cuts[:-1], cuts[1:]))
        ]
        load_w = begin(w_hbm, w_ref, w_sem)
    left32[...] = left_ref[...].astype(F32)
    right32[...] = right_ref[...].astype(F32)

    def put(i, row, left, right):
        pad_ref[0, i] = shifted(row, left, 1)
        pad_ref[1, i] = row
        pad_ref[2, i] = shifted(row, right, -1)

    ends = []
    if start == 0:
        ends.append((0, 0, top_ref))
    if start + rows == total:
        ends.append((1, rows + 1, bottom_ref))
    for side, i, ref in ends:

        @pl.when(inside_ref[side] > 0)
        def _():
            put(i, ref[0:cols, :], ref[cols : cols + 1, :], ref[cols + 8 : cols + 9, :])

        @pl.when(inside_ref[side] == 0)
        def _():
            for b in range(3):
                pad_ref[b, i] = jnp.zeros(pad_ref.shape[2:], BF)

    def fill(i, carry):
        at = pl.ds(base + i, 1)
        put(base + i + 1 - start, grid_ref[i], left32[at, :], right32[at, :])
        return carry

    def fill_rows(i, j):
        def four(k, carry):
            for q in range(4):
                fill(i + 4 * k + q, carry)
            return carry

        lax.fori_loop(0, (j - i) // 4, four, 0)
        for row in range(j - (j - i) % 4, j):
            fill(row, 0)

    for load, i, j in zip(loads, cuts[:-1], cuts[1:]):
        load.wait()
        fill_rows(i, j)
    if not back:
        fill_rows(0, held)
    stores = []
    if back:
        stores += [begin(pad_ref.at[b], pad_hbm.at[b], pad_sem.at[b]) for b in range(3)]
        load_w.wait()

    def store(n):
        return pltpu.make_async_copy(
            out_ref.at[pl.ds(n * high, high)], out_hbm.at[pl.ds(start + n * high, high)], out_sem.at[n]
        )

    def step(n, carry):
        i = n * high
        acc = grid_ref[pl.ds(start - base + i, high)].astype(F32).reshape(high * cols, width)
        for a in range(3):
            for b in range(3):
                part = pad_ref[b, pl.ds(i + a, high)].reshape(high * cols, width)
                tap = a * 3 + b
                acc = acc + (dot(part, w_ref[8 - tap], 1, 1) if back else dot(part, w_ref[tap]))
        out_ref[pl.ds(i, high)] = acc.astype(BF).reshape(high, cols, width)
        store(n).start()
        return carry

    lax.fori_loop(0, blocks, step, 0)
    for n in range(blocks):
        store(n).wait()
    for move in stores:
        move.wait()


def side_edges(last, first):
    count = lax.axis_size("lon")
    up = [(i, (i + 1) % count) for i in range(count)]
    down = [(j, i) for i, j in up]
    return lax.ppermute(last, "lon", up), lax.ppermute(first, "lon", down)


def end_rows(grid, left, right):
    pad = ((0, 7), (0, 0))

    def row(i):
        return jnp.concatenate([grid[i], jnp.pad(left[i][None], pad), jnp.pad(right[i][None], pad)], axis=0)

    return row(grid.shape[0] - 1), row(0)


def end_edges(last, first):
    count = lax.axis_size("lat")
    up = [(i, (i + 1) % count) for i in range(count)]
    down = [(j, i) for i, j in up]
    return lax.ppermute(last, "lat", up), lax.ppermute(first, "lat", down)


def conv(grid, halo, w, back, start=0, stop=None, into=None):
    total, cols, width = grid.shape
    stop = stop or total
    rows = stop - start
    held = min(stop + 1, total) - max(start - 1, 0)
    outs = [shape(grid.shape, BF)]
    pad = (3, rows + 2, cols, width)
    blocks = rows // 8
    scratch = [
        pltpu.VMEM(pad, BF),
        pltpu.VMEM((rows, cols, width), BF),
        pltpu.VMEM((total, width), F32),
        pltpu.VMEM((total, width), F32),
        DMA((blocks,)),
    ]
    if back:
        outs.append(shape(pad, BF))
        scratch = [
            pltpu.VMEM((held, cols, width), BF),
            pltpu.VMEM(w.shape, BF),
            *scratch[:4],
            DMA((blocks + 1,)),
            DMA,
            DMA((blocks,)),
            DMA((3,)),
        ]
    flops = 18 * rows * cols * width * width
    body = functools.partial(conv_body, back=back, start=start, total=total)
    at = lax.axis_index("lat")
    inside = jnp.stack([at > 0, at < lax.axis_size("lat") - 1]).astype(I32)
    args = [inside, grid, *halo, w]
    alias = {}
    if into is not None:
        alias = {len(args): 0}
        args.append(into)
    return kernel_call(
        body, outs, args, flops, scratch, smem=(0,), hbm=(1, 6) if back else (7,), far=(0, 1), temp=8, alias=alias
    )


def gelu_parts(x):
    scale = 0.7978845608028654
    inner = scale * (x + 0.044715 * x * x * x)
    th = jnp.tanh(inner)
    value = 0.5 * x * (1.0 + th)
    slope = 0.5 * (1.0 + th) + 0.5 * x * (1.0 - th * th) * scale * (1.0 + 3 * 0.044715 * x * x)
    return value, slope


def cell_codes(recv_ref, slots):
    owners = recv_ref.shape[0]
    per = 128 // slots
    high, low = [], []
    for p in range(owners // per):
        total = recv_ref[p * per, slots : slots + 8, :].astype(F32)
        for q in range(1, per):
            total = total + recv_ref[p * per + q, slots : slots + 8, :].astype(F32)
        high.append(total[0:1])
        low.append(total[1:2])
    high = jnp.concatenate(high, axis=0)
    low = jnp.concatenate(low, axis=0)
    return (high - 1.0) * 128.0 + low


def gather_body(
    recv_ref, dfield_hbm, w_ref, grad_hbm, eg_hbm, embed_hbm, code_hbm,
    dfield_ref, grad_ref, eg_ref, embed_ref, code_ref, column_ref, slope_ref, in_sem, grad_sem, out_sem, *, slots,
):
    owners = recv_ref.shape[0]
    cells = dfield_ref.shape[0]
    size = 512
    group = size // slots
    blocks = owners // group
    load = begin(dfield_hbm, dfield_ref, in_sem)
    code_ref[...] = cell_codes(recv_ref, slots)
    stores = [begin(code_ref, code_hbm, out_sem.at[0])]

    def features(blk):
        return jnp.concatenate([recv_ref[blk * group + q, :slots, :] for q in range(group)], axis=0)

    codes = code_ref[...].T.astype(I32)
    for p in range(codes.shape[1]):
        column_ref[p * 128 : (p + 1) * 128, :] = codes[:, p : p + 1]

    def activate(blk, carry):
        at = pl.ds(pl.multiple_of(blk * size, size), size)
        value, slope = gelu_parts(dot(features(blk), w_ref[...]))
        embed_ref[at, :] = value.astype(BF)
        slope_ref[at, :] = slope
        return carry

    lax.fori_loop(0, blocks, activate, 0)
    stores.append(begin(embed_ref, embed_hbm, out_sem.at[1]))
    eg_ref[...] = jnp.zeros_like(eg_ref)
    load.wait()

    def store(blk):
        at = pl.ds(pl.multiple_of(blk * size, size), size)
        return pltpu.make_async_copy(grad_ref.at[at], grad_hbm.at[at], grad_sem.at[blk])

    def pick(blk, carry):
        at = pl.ds(pl.multiple_of(blk * size, size), size)
        mask = (iota((size, cells), 1) == column_ref[at, :]).astype(BF)
        rows = dot(mask, dfield_ref[...]).astype(BF)
        grad_ref[at, :] = rows
        store(blk).start()
        dh = rows.astype(F32) * slope_ref[at, :]
        part = dh.astype(BF)
        rest = (dh - part.astype(F32)).astype(BF)
        feat = features(blk)
        eg_ref[...] += dot(feat, part, 0, 0) + dot(feat, rest, 0, 0)
        return carry

    lax.fori_loop(0, blocks, pick, 0)
    stores.append(begin(eg_ref, eg_hbm, out_sem.at[2]))
    for blk in range(blocks):
        store(blk).wait()
    for move in stores:
        move.wait()


def field_body(
    me_ref, code_hbm, embed_hbm, bg_hbm, pad_hbm, eg_hbm, field_hbm, keep_ref, give_ref, last_ref, first_ref,
    code_ref, embed_ref, bg_ref, pad_ref, eg_ref, field_ref, acc_ref, last32, first32, sems, pad_sems, out_sems, bg_sems,
):
    loads = [
        begin(code_hbm, code_ref, sems.at[0]),
        begin(embed_hbm, embed_ref, sems.at[1]),
        begin(pad_hbm.at[:, :2], pad_ref.at[:, :2], sems.at[4]),
    ]
    cells, width = bg_ref.shape
    cols = pad_ref.shape[2]
    half = width // 2
    size = 512
    deep = 2 * size
    high = deep // cols
    blocks = cells // deep

    def load_pad(n):
        some = pl.ds(n * high + 2, high)
        return pltpu.make_async_copy(pad_hbm.at[:, some], pad_ref.at[:, some], pad_sems.at[n])

    def load_bg(n):
        some = pl.ds(pl.multiple_of(n * deep, deep), deep)
        return pltpu.make_async_copy(bg_hbm.at[some], bg_ref.at[some], bg_sems.at[n])

    for n in range(blocks):
        load_bg(n).start()
        load_pad(n).start()
    loads.append(begin(eg_hbm, eg_ref, sems.at[3]))
    acc_ref[...] = jnp.zeros_like(acc_ref)
    for move in loads[:3]:
        move.wait()
    codes = code_ref[...].astype(I32)

    def store(n):
        at = pl.ds(pl.multiple_of(n * deep, deep), deep)
        return pltpu.make_async_copy(field_ref.at[at], field_hbm.at[at], out_sems.at[n])

    def scatter(n):
        for k in range(deep // size):
            base = n * deep + k * size
            where = iota((size, 128), 0) + base
            mask = jnp.concatenate(
                [(where == codes[p : p + 1, :]).astype(BF) for p in range(codes.shape[0])], axis=1
            )
            at = pl.ds(pl.multiple_of(base, size), size)
            total = dot(mask, embed_ref[...]) + bg_ref[at, :].astype(F32)
            field_ref[at, :] = total.astype(BF)
            for g in range(size // cols):
                row = pl.ds(base // cols + g, 1)
                first32[row, :] = total[g * cols : g * cols + 1]
                last32[row, :] = total[(g + 1) * cols - 1 : (g + 1) * cols]
        store(n).start()

    def correlate(n):
        field = field_ref[pl.ds(pl.multiple_of(n * deep, deep), deep), :]
        for a in range(3):
            for b in range(3):
                part = pad_ref[2 - b, pl.ds(n * high + 2 - a, high)].reshape(deep, width)
                acc_ref[3 * a + b] += dot(field, part, 0, 0)

    def step(n, carry):
        load_bg(n).wait()
        scatter(n)
        load_pad(n).wait()
        correlate(n)
        return carry

    lax.fori_loop(0, blocks, step, 0)
    loads[3].wait()
    last_ref[...] = last32[...].astype(BF)
    first_ref[...] = first32[...].astype(BF)
    side = me_ref[0] % 2
    taps = acc_ref.shape[0]
    used = taps * width
    inputs = eg_ref.shape[0]
    for s in range(2):
        lanes = slice(s * half, (s + 1) * half)
        for ref, want in ((keep_ref, s), (give_ref, 1 - s)):

            @pl.when(side == want)
            def _():
                for t in range(taps):
                    ref[t * width : (t + 1) * width, :] = acc_ref[t, :, lanes]
                ref[used : used + inputs, :] = eg_ref[:, lanes]
                if used + inputs < ref.shape[0]:
                    ref[used + inputs :, :] = jnp.zeros((ref.shape[0] - used - inputs, half), F32)

    for n in range(blocks):
        store(n).wait()


def swap(x, bit):
    count = lax.axis_size("lon") * lax.axis_size("lat")
    return lax.ppermute(x, AXES, [(i, i ^ bit) for i in range(count)])


def split_body(mine_ref, *refs, moves, parts):
    n = len(moves)
    ins = refs[: len(refs) - 1 - n]
    keep_ref = refs[len(refs) - 1 - n]
    outs = refs[len(refs) - n :]
    mine = mine_ref[0]

    def put(ref, index):
        row = 0
        for p in range(parts):
            terms = ins[p::parts]
            size = terms[0].shape[0] // (n + 1)
            at = pl.ds(pl.multiple_of(index * size, 8), size)
            total = terms[0][at, :].astype(F32)
            for term in terms[1:]:
                total = total + term[at, :].astype(F32)
            ref[row : row + size, :] = total.astype(ref.dtype)
            row += size

    put(keep_ref, mine)
    for ref, move in zip(outs, moves):
        put(ref, mine ^ move)


def join_body(mine_ref, *refs, parts):
    out_ref = refs[-1]
    ways = len(refs) - 1
    mine = mine_ref[0]
    for move, ref in enumerate(refs[:-1]):
        row, base = 0, 0
        for size in parts:
            at = pl.ds(pl.multiple_of(base + (mine ^ move) * size, 8), size)
            out_ref[at, :] = ref[row : row + size, :]
            row += size
            base += size * ways


def final_body(mine_ref, own_ref, other_ref, conv_ref, embed_ref):
    side = mine_ref[0]
    half = own_ref.shape[1]
    taps, width, _ = conv_ref.shape
    inputs = embed_ref.shape[0]
    for s in range(2):
        lanes = slice(s * half, (s + 1) * half)
        for ref, want in ((own_ref, s), (other_ref, 1 - s)):

            @pl.when(side == want)
            def _():
                for t in range(taps):
                    conv_ref[t, :, lanes] = ref[t * width : (t + 1) * width, :].astype(F32)
                embed_ref[:, lanes] = ref[taps * width : taps * width + inputs, :].astype(F32)


def stages(count):
    bits, found = [], 2
    while found < count:
        bits.append(found)
        found *= 2
    return [bits[i : i + 2] for i in range(0, len(bits), 2)]


def reduce_all(me, keeps, gives, taps, width, inputs, beside, halo_of, encode, unroute):
    count = lax.axis_size("lon") * lax.axis_size("lat")
    terms = [*keeps, *(swap(x, 1) for x in gives)]
    half = width // 2
    plan = stages(count)
    sizes = []
    for bits in plan:
        ways = 2 ** len(bits)
        parts = len(keeps) if bits is plan[0] else 1
        sizes.append([x.shape[0] // ways for x in terms[:parts]])
        mine = (me // bits[0]) % ways
        moves = list(range(1, ways))
        outs = [shape((sum(sizes[-1]), half), F32)] + [shape((sum(sizes[-1]), half), BF)] * len(moves)
        body = functools.partial(split_body, moves=moves, parts=parts)
        own, *send = kernel_call(body, outs, (mine, *terms), smem=(0,))
        if bits is plan[0]:
            send, edges = lax.optimization_barrier((send, beside[1]))
            halo = halo_of(edges)
        terms = [own] + [swap(x, m * bits[0]) for m, x in zip(moves, send)]
        if bits is plan[0]:
            terms, back = lax.optimization_barrier((terms, beside[0]))
        if bits is plan[-1]:
            terms, gone = lax.optimization_barrier((terms, unroute(back)))
    body = functools.partial(split_body, moves=[], parts=1)
    (block,) = kernel_call(
        body, [shape(terms[0].shape, BF)], (jnp.zeros((1,), I32), *terms), smem=(0,)
    )
    for bits, parts in zip(reversed(plan), reversed(sizes)):
        ways = 2 ** len(bits)
        mine = (me // bits[0]) % ways
        pieces = [block] + [swap(block, m * bits[0]) for m in range(1, ways)]
        if bits is plan[-1]:
            pieces, found = lax.optimization_barrier((pieces, encode(halo, 0, None)))
        if bits is plan[0]:
            pieces, found = lax.optimization_barrier((pieces, encode(halo, 1, found)))
        rows = block.shape[0]
        body = functools.partial(join_body, parts=parts)
        (block,) = kernel_call(body, [shape((rows * ways, half), BF)], (mine, *pieces), smem=(0,))
    other = swap(block, 1)
    outs = [shape((taps, width, width), F32), shape((inputs, width), F32)]
    return kernel_call(final_body, outs, (me % 2, block, other), smem=(0,)), found, gone


def on_device(obs_feat, obs_tile, obs_cell, w_embed, background, w_conv, cotangent):
    lon_count = lax.axis_size("lon")
    lat_count = lax.axis_size("lat")
    owners = lon_count * lat_count
    records, inputs = obs_feat.shape
    slots = 2 * records // owners
    rows, cols, width = background.shape
    cells = rows * cols
    taps = w_conv.shape[0]
    me = (lax.axis_index("lon") * lat_count + lax.axis_index("lat")).astype(I32).reshape(1)

    outs = [shape((owners, slots + 8, inputs), BF), shape((1, records), I32)]
    send, place = kernel_call(
        functools.partial(route_body, owners=owners, slots=slots),
        outs,
        (me, obs_tile.reshape(1, records), obs_cell.reshape(1, records), obs_feat),
        flops=4 * records * records * inputs,
        scratch=[
            pltpu.VMEM((512, records), BF),
            pltpu.VMEM((1, records), I32),
            pltpu.VMEM((1, records), I32),
            pltpu.VMEM((records, inputs), BF),
            DMA((3,)),
        ],
        smem=(0,),
        hbm=(1, 2, 3),
        temp=4,
    )
    sides = side_edges(cotangent[:, cols - 1], cotangent[:, 0])
    send, sides = lax.optimization_barrier((send, sides))
    ends = end_rows(cotangent, *sides)
    send, ends = lax.optimization_barrier((send, ends))
    halo = (*sides, *end_edges(*ends))
    recv = lax.all_to_all(send, AXES, split_axis=0, concat_axis=0, tiled=True)

    dfield, pad = conv(cotangent, halo, w_conv, True)

    count = owners * slots
    grad, local_eg, embed, codes = kernel_call(
        functools.partial(gather_body, slots=slots),
        [
            shape((count, width), BF),
            shape((inputs, width), F32),
            shape((count, width), BF),
            shape((count // 128, 128), F32),
        ],
        (recv, dfield.reshape(cells, width), w_embed),
        flops=2 * count * cells * width,
        scratch=[
            pltpu.VMEM((cells, width), BF),
            pltpu.VMEM((count, width), BF),
            pltpu.VMEM((inputs, width), F32),
            pltpu.VMEM((count, width), BF),
            pltpu.VMEM((count // 128, 128), F32),
            pltpu.VMEM((count, 1), I32),
            pltpu.VMEM((count, width), F32),
            DMA,
            DMA((count // 512,)),
            DMA((3,)),
        ],
        hbm=(1,),
        far=(0, 1, 2, 3),
        temp=12,
    )
    blocks = owners // 2
    size = 8 * blocks
    total = -(-(taps * width + inputs) // size) * size
    back = lax.all_to_all(grad.reshape(owners, slots, width), AXES, split_axis=0, concat_axis=0, tiled=True)
    field, keep, give, last, first = kernel_call(
        field_body,
        [shape((cells, width), BF)]
        + [shape((total, width // 2), F32)] * 2
        + [shape((rows, width), BF)] * 2,
        (me, codes, embed, background.reshape(cells, width), pad, local_eg),
        flops=2 * count * cells * width + 18 * cells * width * width,
        scratch=[
            pltpu.VMEM((count // 128, 128), F32),
            pltpu.VMEM((count, width), BF),
            pltpu.VMEM((cells, width), BF),
            pltpu.VMEM(pad.shape, BF),
            pltpu.VMEM((inputs, width), F32),
            pltpu.VMEM((cells, width), BF),
            pltpu.VMEM((taps, width, width), F32),
            pltpu.VMEM((rows, width), F32),
            pltpu.VMEM((rows, width), F32),
            DMA((5,)),
            DMA((cells // 1024,)),
            DMA((cells // 1024,)),
            DMA((cells // 1024,)),
        ],
        smem=(0,),
        hbm=(1, 2, 3, 4, 5),
        far=(0,),
        temp=8,
    )
    grid = field.reshape(rows, cols, width)

    def halo_of(edges):
        sides = side_edges(*edges)
        return (*sides, *end_edges(*end_rows(grid, *sides)))

    def encode(halo, part, into):
        cuts = (0, rows // 2, rows)
        return conv(grid, halo, w_conv, False, cuts[part], cuts[part + 1], into)[0]

    def unroute(back):
        return kernel_call(
            unroute_body,
            [shape((records, width), BF)],
            (place, back.reshape(count, width)),
            flops=2 * count * records * width,
            temp=4,
        )[0]

    (conv_grad, embed_grad), encoded, record_grad = reduce_all(
        me, (keep,), (give,), taps, width, inputs, (back, (last, first)), halo_of, encode, unroute
    )
    return encoded, record_grad, conv_grad, embed_grad


def solution(mesh):
    placed = (
        P(("lon", "lat"), None),
        P(("lon", "lat"), None),
        P(("lon", "lat")),
        P(),
        P("lat", "lon", None),
        P(),
        P("lat", "lon", None),
    )
    return jax.shard_map(
        on_device,
        mesh=mesh,
        in_specs=placed,
        out_specs=(P("lat", "lon", None), P(("lon", "lat"), None), P(), P()),
        check_vma=False,
    )
```
